128 devices in a mesh: section: 2 (over y_lo), gx: 8 (over z, y_hi), gy: 8 (over x, core).
Axes of the slice: x: 4, y: 4 (y_hi: 2, y_lo: 2; y = y_hi * 2 + y_lo), z: 4, core: 2. Of those that a mesh axis runs over, the one named last changes fastest.
Arguments:
- fields: float32 [2, 4, 64, 512, 2048], P('section', None, None, 'gx', 'gy'), may hold values from -6 to 6
- slot_pick: int32 [4], replicated, may hold values from 0 to 3, each once
- courant_x: float32 [64, 512, 2048], P(None, 'gx', 'gy'), may hold values from 0.05 to 0.3
- courant_y: float32 [64, 512, 2048], P(None, 'gx', 'gy'), may hold values from 0.05 to 0.3
- horiz_diff: float32 [64], replicated, may hold values from 0.01 to 0.05
- vert_diff: float32 [64], replicated, may hold values from 0.01 to 0.1
- precip_class: int32 [512, 2048], P('gx', 'gy'), may hold values from 0 to 3
- class_rates: float32 [4], replicated, may hold values from 0.05 to 0.6
- vent_cells: int32 [64], replicated, may hold values from 0 to 1048575
- vent_rate: float32 [64], replicated, may hold values from 0.5 to 2
- profile: float32 [64], replicated, may hold values from 0.05 to 1
Outputs:
- window_fields: float32 [2, 64, 512, 2048], P('section', None, 'gx', 'gy')
- sensitivity: float32 [64], replicated
The draws below stay inside these ranges and needn't reach their ends.
Inputs may be any that keep to these rules, and one draw needn't show every extreme that they name: `slot_pick`: each slot number appears once.
All inputs are finite; a program needn't handle non-finite values.
Results may differ from the reference program's by a relative error of at most 0.000088.
Values sent between devices are 32-bit elements; how exact they have to be, the bound alone decides.
A program may use at most 192 MiB of HBM per device.

```python
import math
import jax
import jax.numpy as jnp

NZ = 64
SLOTS = 4
CLASSES = 4
VENTS = 64
NX = 512
NY = 2048


def touch_ends(entries, rng, smallest, high):
    longest = entries.shape.index(max(entries.shape))
    spots = []
    for shift in (0, 1):
        where = [jax.random.randint(jax.random.fold_in(rng, axis), (), 0, length) for axis, length in enumerate(entries.shape)]
        where[longest] = (where[longest] + shift) % entries.shape[longest]
        spots.append(tuple(where))
    return entries.at[spots[0]].set(smallest).at[spots[1]].set(high)


def level_of(own_key, shape, pieces, smallest, largest):
    gain = 1.0
    for dim, shards_of in pieces:
        draws = jax.random.uniform(jax.random.fold_in(jax.random.fold_in(own_key, 6), dim), (shards_of,), jnp.float32, smallest / len(pieces), largest / len(pieces))
        gain = gain * jnp.repeat(jnp.exp(draws), shape[dim] // shards_of).reshape((-1,) + (1,) * (len(shape) - 1 - dim))
    return gain


def scatter_about(key, shape, width, reach, cuts=(), held_as=jnp.bfloat16):
    factor_of = level_of(key, shape, cuts, -0.22, 0.18) if cuts else 1.0
    entries = jax.random.normal(key, shape, jnp.float32) * width * factor_of
    return jnp.minimum(jnp.maximum(entries, -reach), reach).astype(held_as)


def setup_inputs(seed: int = 0) -> dict:
    splits = jax.random.split(jax.random.key(seed), 12)
    return {
        "fields": scatter_about(splits[0], (2, SLOTS, NZ, NX, NY), 1.0, 6.0, ((0, 2), (3, 8), (4, 8)), jnp.float32),
        "slot_pick": jax.random.permutation(splits[1], SLOTS).astype(jnp.int32),
        "courant_x": jnp.clip(0.05 + 0.25 * jax.random.uniform(splits[2], (NZ, NX, NY), jnp.float32) ** level_of(splits[2], (NZ, NX, NY), ((1, 8), (2, 8)), -0.2, 0.2), 0.05, 0.3),
        "courant_y": jnp.clip(0.05 + 0.25 * jax.random.uniform(splits[3], (NZ, NX, NY), jnp.float32) ** level_of(splits[3], (NZ, NX, NY), ((1, 8), (2, 8)), -0.2, 0.2), 0.05, 0.3),
        "horiz_diff": jnp.clip(jnp.exp(jax.random.uniform(splits[4], (NZ,), jnp.float32, math.log(0.01), math.log(0.05))), 0.01, 0.05),
        "vert_diff": jnp.clip(jnp.exp(jax.random.uniform(splits[5], (NZ,), jnp.float32, math.log(0.01), math.log(0.1))), 0.01, 0.1),
        "precip_class": touch_ends(jax.random.randint(splits[6], (NX, NY), 0, CLASSES), jax.random.fold_in(splits[6], 1), 0, CLASSES - 1).astype(jnp.int32),
        "class_rates": jnp.clip(jnp.exp(jax.random.uniform(splits[7], (CLASSES,), jnp.float32, math.log(0.05), math.log(0.6))), 0.05, 0.6),
        "vent_cells": touch_ends(jax.random.randint(splits[8], (VENTS,), 0, NX * NY), jax.random.fold_in(splits[8], 1), 0, (NX * NY) - 1).astype(jnp.int32),
        "vent_rate": jnp.clip(jax.random.uniform(splits[9], (VENTS,), jnp.float32, 0.5, 2.0), 0.5, 2.0),
        "profile": jnp.clip(jnp.exp(jax.random.uniform(splits[10], (NZ,), jnp.float32, math.log(0.05), math.log(1.0))), 0.05, 1.0),
    }


def wash(conc):
    return conc * conc / (1.0 + conc * conc)


def slope(conc):
    denom = 1.0 + conc * conc
    return 2.0 * conc / (denom * denom)


def spread(padded, coefs):
    west_coef, east_coef, south_coef, north_coef, above_coef, below_coef, diag_coef = coefs
    total = diag_coef * padded[1:-1, 1:-1, 1:-1]
    total = total + west_coef * padded[1:-1, :-2, 1:-1] + east_coef * padded[1:-1, 2:, 1:-1]
    total = total + south_coef * padded[1:-1, 1:-1, :-2] + north_coef * padded[1:-1, 1:-1, 2:]
    total = total + above_coef * padded[2:, 1:-1, 1:-1] + below_coef * padded[:-2, 1:-1, 1:-1]
    return total


def reference(fields, slot_pick, courant_x, courant_y, horiz_diff, vert_diff, precip_class, class_rates, vent_cells, vent_rate, profile):
    start = fields[0, slot_pick[0]]
    lam_two = fields[1, slot_pick[1]]
    horiz = horiz_diff[:, None, None]
    vertical = vert_diff[:, None, None]
    zero_one = jnp.zeros((1,), jnp.float32)
    kd_above = jnp.concatenate([vert_diff[1:], zero_one])[:, None, None]
    kd_below = jnp.concatenate([zero_one, vert_diff[:-1]])[:, None, None]
    diag_coef = 1.0 - courant_x - courant_y - 4.0 * horiz - 2.0 * vertical
    cu_next = jnp.concatenate([courant_x[:, 1:, :], jnp.zeros((NZ, 1, NY), jnp.float32)], 1)
    cv_next = jnp.concatenate([courant_y[:, :, 1:], jnp.zeros((NZ, NX, 1), jnp.float32)], 2)
    flat_h = horiz + 0.0 * courant_x
    fwd_coefs = (courant_x + horiz, flat_h, courant_y + horiz, flat_h, vertical + 0.0 * courant_x, vertical + 0.0 * courant_x, diag_coef)
    adj_coefs = (flat_h, cu_next + horiz, flat_h, cv_next + horiz, kd_above + 0.0 * courant_x, kd_below + 0.0 * courant_x, diag_coef)
    rate = class_rates[precip_class]
    column = jnp.zeros((NX * NY,), jnp.float32).at[vent_cells].add(vent_rate).reshape(NX, NY)
    emission = profile[:, None, None] * column

    def padit(field):
        return jnp.pad(field, ((1, 1), (1, 1), (1, 1)))

    conc_one = spread(padit(start), fwd_coefs) - rate * wash(start) + emission
    conc_two = spread(padit(conc_one), fwd_coefs) - rate * wash(conc_one) + emission
    lam_one = spread(padit(lam_two), adj_coefs) - rate * slope(conc_one) * lam_two
    lam_zero = spread(padit(lam_one), adj_coefs) - rate * slope(start) * lam_one
    colsum = jnp.sum(profile[:, None, None] * (lam_one + lam_two), 0).reshape(-1)
    sensitivity = colsum[vent_cells]
    return jnp.stack([conc_two, lam_zero]), sensitivity
```

```python
import functools

import jax
import jax.numpy as jnp
from jax import lax
from jax.experimental import pallas as pl
from jax.experimental.pallas import tpu as pltpu
from jax.sharding import PartitionSpec as P

MESH = pl.DeviceIdType.MESH
LANES = 128
CHUNK = 4
N_LONG = 20
FIRST_LONG = 4


def wash_and_slope(conc):
    square = conc * conc
    inverse = 1.0 / (1.0 + square)
    return square * inverse, 2.0 * conc * inverse * inverse


def kernel(
    fields_ref,
    cx_ref,
    cy_ref,
    pick_ref,
    h_ref,
    k_ref,
    rates_ref,
    cells_ref,
    vent_ref,
    prof_ref,
    class_ref,
    out_ref,
    terms_ref,
    slots,
    c0,
    lam2,
    cx,
    cy,
    state,
    long_buf,
    rate,
    column,
    colsum,
    pack_f,
    pack_c,
    pack_m,
    pack_out,
    edge_hi,
    edge_lo,
    edge_f0,
    edge_c0,
    edge_mhi,
    edge_mlo,
    got_w,
    got_e,
    got_xw,
    got_xe,
    part_p,
    part_hi,
    part_lo,
    halo,
    ld_sem,
    st_sem,
    c0_send,
    c0_recv,
    lg_send,
    lg_recv,
    hx_send,
    hx_recv,
    pt_send,
    pt_recv,
):
    nz, nr, nc = c0.shape
    n_chunks = nz // CHUNK
    s = lax.axis_index("section")
    gx = lax.axis_index("gx")
    gy = lax.axis_index("gy")
    ngx, ngy = lax.axis_size("gx"), lax.axis_size("gy")
    half = (nr, LANES)
    lane = lax.broadcasted_iota(jnp.int32, half, 1)
    row = lax.broadcasted_iota(jnp.int32, half, 0)
    halves = (slice(0, LANES), slice(LANES, 2 * LANES))

    partner = {"section": 1 - s}
    cross = {"section": 1 - s, "gx": gx + 1 - 2 * lax.rem(gx, 2)}
    beside = (
        {"gy": lax.rem(gy + 1, ngy)},
        {"gy": lax.rem(gy + ngy - 1, ngy)},
        {"gx": lax.rem(gx + 1, ngx)},
        {"gx": lax.rem(gx + ngx - 1, ngx)},
    )

    def remote(src, dst, send, recv, to):
        return pltpu.make_async_remote_copy(
            src, dst, send, recv, device_id=to, device_id_type=MESH
        )

    def loads(i):
        at = pl.ds(i * CHUNK, CHUNK)
        return (
            pltpu.make_async_copy(fields_ref.at[0, :, at], slots.at[:, at], ld_sem.at[0, i]),
            pltpu.make_async_copy(cx_ref.at[at], cx.at[at], ld_sem.at[1, i]),
            pltpu.make_async_copy(cy_ref.at[at], cy.at[at], ld_sem.at[2, i]),
        )

    def store(i):
        at = pl.ds(i * CHUNK, CHUNK)
        return pltpu.make_async_copy(cx.at[at], out_ref.at[at], st_sem.at[i])

    def direct(z):
        return remote(c0.at[z], c0.at[z], c0_send.at[z], c0_recv.at[z], partner)

    def long_plane(j):
        return FIRST_LONG + 3 * j

    def long_one(j):
        z = long_plane(j)
        return remote(c0.at[z], long_buf.at[j], c0_send.at[z], lg_recv.at[j], cross)

    def long_two(j):
        return remote(long_buf.at[j], long_buf.at[j], lg_send.at[j], lg_recv.at[j], partner)

    def long_three(j):
        z = long_plane(j)
        return remote(long_buf.at[j], c0.at[z], lg_send.at[j], c0_recv.at[z], cross)

    def exchange(e):
        return (
            remote(pack_out.at[e], got_w.at[e], hx_send.at[e, 0], hx_recv.at[e, 0], beside[0]),
            remote(pack_out.at[e], got_e.at[e], hx_send.at[e, 1], hx_recv.at[e, 1], beside[1]),
            remote(edge_hi.at[e], got_xw.at[e], hx_send.at[e, 2], hx_recv.at[e, 2], beside[2]),
            remote(edge_lo.at[e], got_xe.at[e], hx_send.at[e, 3], hx_recv.at[e, 3], beside[3]),
        )

    def to_partner():
        return (
            remote(pack_out.at[1], part_p, pt_send.at[0], pt_recv.at[0], partner),
            remote(edge_hi.at[1], part_hi, pt_send.at[1], pt_recv.at[1], partner),
            remote(edge_lo.at[1], part_lo, pt_send.at[2], pt_recv.at[2], partner),
        )

    def finish_exchange(e):
        for copy in exchange(e):
            copy.wait_recv()
        west = jnp.where(gy > 0, 1.0, 0.0)
        east = jnp.where(gy < ngy - 1, 1.0, 0.0)
        low = jnp.where(gx > 0, 1.0, 0.0)
        high = jnp.where(gx < ngx - 1, 1.0, 0.0)
        moved = pltpu.roll(got_e[e], LANES - 2, 1)
        halo[...] = jnp.where(lax.rem(lane, 2) == 0, got_w[e] * west, moved * east)
        got_xw[e] = got_xw[e] * low
        got_xe[e] = got_xe[e] * high

    def pack(ref, z, left, right, *at):
        both = pltpu.roll(jnp.where(lane == LANES - 1, right, left), 2 * z + 1, 1)
        where = (*at, slice(None), slice(None))
        ref[where] = jnp.where(lane // 2 == z, both, ref[where])

    def neighbours(z, e, f, gxs, gys):
        side = pltpu.roll(halo[...], lax.rem(2 * nz - 2 * z, LANES), 1)
        lo = [pltpu.roll(a, 1, 1) for a in f]
        hi = [pltpu.roll(a, LANES - 1, 1) for a in gys]
        south = (jnp.where(lane == 0, side, lo[0]), jnp.where(lane == 0, lo[0], lo[1]))
        north = (
            jnp.where(lane == LANES - 1, hi[1], hi[0]),
            jnp.where(lane == LANES - 1, side, hi[1]),
        )
        below = [got_xw[e, z, :, at] for at in halves]
        above = [got_xe[e, z, :, at] for at in halves]
        west = [jnp.where(row == 0, b, pltpu.roll(a, 1, 0)) for a, b in zip(f, below)]
        east = [jnp.where(row == nr - 1, b, pltpu.roll(a, nr - 1, 0)) for a, b in zip(gxs, above)]
        return west, east, south, north

    def read(ref, z):
        return [ref[z, :, at] for at in halves]

    def vertical(z):
        up, down = jnp.minimum(z + 1, nz - 1), jnp.maximum(z - 1, 0)
        return up, down, jnp.where(z < nz - 1, 1.0, 0.0), jnp.where(z > 0, 1.0, 0.0)

    def forward(src, z, e):
        f, u, v = read(src, z), read(cx, z), read(cy, z)
        h, k = h_ref[z], k_ref[z]
        if e is None:
            west = [pltpu.roll(a, 1, 0) for a in f]
            east = [pltpu.roll(a, nr - 1, 0) for a in f]
            lo = [pltpu.roll(a, 1, 1) for a in f]
            hi = [pltpu.roll(a, LANES - 1, 1) for a in f]
            south = (lo[0], jnp.where(lane == 0, lo[0], lo[1]))
            north = (jnp.where(lane == LANES - 1, hi[1], hi[0]), hi[1])
        else:
            west, east, south, north = neighbours(z, e, f, f, f)
        up, down, has_up, has_down = vertical(z)
        above, below = read(src, up), read(src, down)
        level = 1.0 - 4.0 * h - 2.0 * k
        out = []
        for i, at in enumerate(halves):
            total = (level - u[i] - v[i]) * f[i] + u[i] * west[i] + v[i] * south[i]
            total = total + h * ((west[i] + east[i]) + (south[i] + north[i]))
            total = total + (k * has_up) * above[i] + (k * has_down) * below[i]
            washed, _ = wash_and_slope(f[i])
            out.append(total - rate[:, at] * washed + prof_ref[z] * column[:, at])
        return out

    def transposed(src, z, e):
        f, u, v = read(src, z), read(cx, z), read(cy, z)
        h, k = h_ref[z], k_ref[z]
        qx = [(b + h) * a for a, b in zip(f, u)]
        qy = [(b + h) * a for a, b in zip(f, v)]
        west, east, south, north = neighbours(z, e, f, qx, qy)
        up, down, has_up, has_down = vertical(z)
        above, below = read(src, up), read(src, down)
        k_up, k_down = k_ref[up] * has_up, k_ref[down] * has_down
        level = 1.0 - 4.0 * h - 2.0 * k
        out = []
        for i in range(2):
            total = (level - u[i] - v[i]) * f[i] + east[i] + north[i] + h * (west[i] + south[i])
            out.append(total + k_up * above[i] + k_down * below[i])
        return out

    def selected(z):
        pick = jnp.full(half, pick_ref[s], jnp.int32)
        out = []
        for at in halves:
            a = jnp.where(pick == 0, slots[0, z, :, at], slots[1, z, :, at])
            b = jnp.where(pick == 2, slots[2, z, :, at], slots[3, z, :, at])
            out.append(jnp.where(pick < 2, a, b))
        return out

    def prepare_columns():
        kind = class_ref[...]
        value = jnp.full(kind.shape, rates_ref[0], jnp.float32)
        for c in range(1, rates_ref.shape[0]):
            value = jnp.where(kind == c, rates_ref[c], value)
        rate[...] = value
        column[...] = jnp.zeros_like(column)

        @pl.loop(0, cells_ref.shape[0])
        def _(v):
            column[...] += jnp.where(cell_ids() == cells_ref[v], vent_ref[v], 0.0)

    def cell_ids():
        rows = lax.broadcasted_iota(jnp.int32, (nr, nc), 0) + gx * nr
        return rows * (nc * ngy) + lax.broadcasted_iota(jnp.int32, (nr, nc), 1) + gy * nc

    @pl.loop(0, n_chunks)
    def _(i):
        for copy in loads(i):
            copy.start()

    barrier = pltpu.get_barrier_semaphore()
    for peer in (partner, cross, *beside):
        pl.semaphore_signal(barrier, 1, device_id=peer, device_id_type=MESH)
    pl.semaphore_wait(barrier, 6)

    @pl.when(s == 0)
    def _():
        def relay(j):
            long_two(j).wait_recv()
            long_three(j).start()

        @pl.loop(0, n_chunks)
        def _(i):
            for copy in loads(i):
                copy.wait()

            @pl.loop(0, CHUNK)
            def _(t):
                z = i * CHUNK + t
                f = selected(z)
                for at, value in zip(halves, f):
                    c0[z, :, at] = value
                    edge_hi[0, z, :, at] = value[nr - 1 : nr]
                    edge_lo[0, z, :, at] = value[0:1]
                pack(pack_out, z, f[0], f[1], 0)
                place = z - FIRST_LONG
                is_long = (
                    (place >= 0) & (place < 3 * N_LONG) & (lax.rem(place + 3 * nz, 3) == 0)
                )

                @pl.when(is_long)
                def _():
                    long_one((place + 3 * nz) // 3 - nz).start()

                @pl.when(jnp.logical_not(is_long))
                def _():
                    direct(z).start()

        for copy in exchange(0):
            copy.start()
        prepare_columns()
        finish_exchange(0)

        @pl.loop(0, nz)
        def _(z):
            new = forward(c0, z, 0)
            for at, value in zip(halves, new):
                state[z, :, at] = value
                edge_hi[1, z, :, at] = value[nr - 1 : nr]
                edge_lo[1, z, :, at] = value[0:1]
            pack(pack_out, z, new[0], new[1], 1)

            @pl.when(lax.rem(z, 8) == 7)
            def _():
                relay(z // 8)

        for copy in (*to_partner(), *exchange(1)):
            copy.start()
        finish_exchange(1)

        @pl.loop(0, nz)
        def _(z):
            new = forward(state, z, 1)
            for at, value in zip(halves, new):
                cx[z, :, at] = value

            @pl.when(lax.rem(z, CHUNK) == CHUNK - 1)
            def _():
                store(z // CHUNK).start()

            @pl.when((lax.rem(z, 4) == 3) & (z // 4 + nz // 8 < N_LONG))
            def _():
                relay(z // 4 + nz // 8)

        terms_ref[...] = jnp.zeros_like(terms_ref)

        @pl.loop(0, N_LONG)
        def _(j):
            long_three(j).wait_send()

        @pl.loop(0, nz)
        def _(z):
            direct(z).wait_send()

        for copy in (*to_partner(), *exchange(0), *exchange(1)):
            copy.wait_send()

        @pl.loop(0, n_chunks)
        def _(i):
            store(i).wait()

    @pl.when(s == 1)
    def _():
        def relay(j):
            long_one(j).wait_recv()
            long_two(j).start()

        @pl.loop(0, n_chunks)
        def _(i):
            for copy in loads(i):
                copy.wait()

            @pl.loop(0, CHUNK)
            def _(t):
                z = i * CHUNK + t
                f = selected(z)
                h = h_ref[z]
                for at, value in zip(halves, f):
                    lam2[z, :, at] = value
                    first = value[0:1]
                    coef = cx[z, 0:1, at] + h
                    edge_hi[0, z, :, at] = value[nr - 1 : nr]
                    edge_lo[0, z, :, at] = coef * first
                    edge_f0[z, :, at] = first
                    edge_c0[z, :, at] = coef
                pack(pack_f, z, f[0], f[1])
                pack(pack_c, z, cy[z, :, 0:LANES] + h, jnp.ones(half, jnp.float32))

        pack_out[0] = pack_f[...] * pack_c[...]
        for copy in exchange(0):
            copy.start()
        for j in range(3):
            relay(j)
        prepare_columns()
        finish_exchange(0)

        @pl.loop(0, nz)
        def _(z):
            new = transposed(lam2, z, 0)
            for at, value in zip(halves, new):
                state[z, :, at] = value
                edge_mhi[z, :, at] = value[nr - 1 : nr]
                edge_mlo[z, :, at] = value[0:1]
            pack(pack_m, z, new[0], new[1])

            @pl.when(lax.rem(z, 8) == 7)
            def _():
                relay(z // 8 + 3)

        colsum[...] = jnp.zeros_like(colsum)
        for copy in to_partner():
            copy.wait_recv()
        _, slope = wash_and_slope(part_hi[...])
        edge_hi[1] = edge_mhi[...] - rate[nr - 1 : nr, :] * slope * edge_hi[0]
        _, slope = wash_and_slope(part_lo[...])
        edge_mlo[...] = edge_mlo[...] - rate[0:1, :] * slope * edge_f0[...]
        edge_lo[1] = edge_mlo[...] * edge_c0[...]
        side_rate = jnp.where(
            lax.rem(lane, 2) == 0,
            jnp.broadcast_to(rate[:, nc - 1 : nc], half),
            jnp.broadcast_to(rate[:, 0:1], half),
        )
        _, slope = wash_and_slope(part_p[...])
        pack_m[...] = pack_m[...] - side_rate * slope * pack_f[...]
        pack_out[1] = pack_m[...] * pack_c[...]
        for copy in exchange(1):
            copy.start()
        for j in range(3 + nz // 8, 3 + nz // 8 + 3):
            relay(j)
        early = 6 + nz // 8
        finish_exchange(1)

        def last(z):
            lam = read(state, z)
            new = transposed(state, z, 1)
            conc = read(c0, z)
            for i, at in enumerate(halves):
                _, bend = wash_and_slope(conc[i])
                cx[z, :, at] = new[i] - rate[:, at] * bend * lam[i]

            @pl.when(lax.rem(z, CHUNK) == CHUNK - 1)
            def _():
                store(z // CHUNK).start()

        direct(0).wait_recv()

        @pl.loop(0, nz)
        def _(z):
            @pl.when(z + early < N_LONG)
            def _():
                relay(z + early)

            @pl.when(z < nz - 1)
            def _():
                direct(z + 1).wait_recv()

            conc = forward(c0, z, None)
            old, field = read(state, z), read(lam2, z)
            sides = pltpu.roll(pack_m[...], lax.rem(2 * nz - 2 * z + LANES - 1, LANES), 1)
            keep = (lane == 0, lane == LANES - 1)
            for i, at in enumerate(halves):
                _, bend = wash_and_slope(conc[i])
                lam = old[i] - rate[:, at] * bend * field[i]
                lam = jnp.where(keep[i], sides, lam)
                lam = jnp.where(row == 0, edge_mlo[z, :, at], lam)
                lam = jnp.where(row == nr - 1, edge_hi[1, z, :, at], lam)
                state[z, :, at] = lam
                colsum[:, at] += prof_ref[z] * (lam + field[i])

            @pl.when(z > 0)
            def _():
                last(z - 1)

        last(nz - 1)

        @pl.loop(0, cells_ref.shape[0])
        def _(v):
            own = jnp.where(cell_ids() == cells_ref[v], colsum[...], 0.0)
            own = own[:, 0:LANES] + own[:, LANES:]
            terms_ref[v] = jnp.sum(own, 0, keepdims=True)

        @pl.loop(0, N_LONG)
        def _(j):
            long_two(j).wait_send()

        for copy in (*exchange(0), *exchange(1)):
            copy.wait_send()

        @pl.loop(0, n_chunks)
        def _(i):
            store(i).wait()


def shards(
    fields,
    slot_pick,
    courant_x,
    courant_y,
    horiz_diff,
    vert_diff,
    precip_class,
    class_rates,
    vent_cells,
    vent_rate,
    profile,
):
    nz, nr, nc = courant_x.shape
    vents = vent_cells.shape[0]
    anywhere = pl.BlockSpec(memory_space=pl.ANY)
    scalars = pl.BlockSpec(memory_space=pltpu.SMEM)
    vector = pl.BlockSpec(memory_space=pltpu.VMEM)
    f32 = jnp.float32
    plane = pltpu.VMEM((nz, nr, nc), f32)
    tile = pltpu.VMEM((nr, nc), f32)
    packed = pltpu.VMEM((nr, LANES), f32)
    edge = pltpu.VMEM((nz, 1, nc), f32)
    packed2 = pltpu.VMEM((2, nr, LANES), f32)
    edge2 = pltpu.VMEM((2, nz, 1, nc), f32)
    dma = pltpu.SemaphoreType.DMA
    window, terms = pl.pallas_call(
        kernel,
        out_shape=(
            jax.ShapeDtypeStruct((nz, nr, nc), f32),
            jax.ShapeDtypeStruct((vents, 1, LANES), f32),
        ),
        in_specs=[anywhere] * 3 + [scalars] * 7 + [vector],
        out_specs=(anywhere, vector),
        scratch_shapes=[
            pltpu.VMEM((fields.shape[1], nz, nr, nc), f32),
            plane,
            plane,
            plane,
            plane,
            plane,
            pltpu.VMEM((N_LONG, nr, nc), f32),
            tile,
            tile,
            tile,
            packed,
            packed,
            packed,
            packed2,
            edge2,
            edge2,
            edge,
            edge,
            edge,
            edge,
            packed2,
            packed2,
            edge2,
            edge2,
            packed,
            edge,
            edge,
            packed,
            dma((3, nz // CHUNK)),
            dma((nz // CHUNK,)),
            dma((nz,)),
            dma((nz,)),
            dma((N_LONG,)),
            dma((N_LONG,)),
            dma((2, 4)),
            dma((2, 4)),
            dma((3,)),
            dma((3,)),
        ],
        compiler_params=pltpu.CompilerParams(
            collective_id=0, has_side_effects=True, vmem_limit_bytes=58 << 20
        ),
    )(
        fields,
        courant_x,
        courant_y,
        slot_pick,
        horiz_diff,
        vert_diff,
        class_rates,
        vent_cells,
        vent_rate,
        profile,
        precip_class,
    )
    sensitivity = lax.psum(jnp.sum(terms, (1, 2)), ("section", "gx", "gy"))
    return window[None], sensitivity


def solution(mesh):
    placed = (
        P("section", None, None, "gx", "gy"),
        P(),
        P(None, "gx", "gy"),
        P(None, "gx", "gy"),
        P(),
        P(),
        P("gx", "gy"),
        P(),
        P(),
        P(),
        P(),
    )
    return jax.shard_map(
        shards,
        mesh=mesh,
        in_specs=placed,
        out_specs=(P("section", None, "gx", "gy"), P()),
        check_vma=False,
    )
```

```python
import jax
import jax.numpy as jnp
from jax import lax
from jax.experimental import pallas as pl
from jax.experimental.pallas import tpu as pltpu
from jax.sharding import PartitionSpec as P

MESH = pl.DeviceIdType.MESH
LANES = 128
CHUNK = 4
N_LONG = 20
EARLY_LONG = 3


def wash_and_slope(conc):
    square = conc * conc
    inverse = 1.0 / (1.0 + square)
    return square * inverse, 2.0 * conc * inverse * inverse


def kernel(
    fields_ref,
    cx_ref,
    cy_ref,
    pick_ref,
    h_ref,
    k_ref,
    rates_ref,
    cells_ref,
    vent_ref,
    prof_ref,
    class_ref,
    where_ref,
    out_ref,
    sums_ref,
    slots,
    c0,
    lam2,
    cx,
    cy,
    state,
    long_buf,
    rate,
    column,
    colsum,
    pack_f,
    pack_c,
    pack_m,
    pack_out,
    edge_hi,
    edge_lo,
    edge_f0,
    edge_c0,
    edge_mhi,
    edge_mlo,
    got_w,
    got_e,
    got_xw,
    got_xe,
    part_p,
    part_hi,
    part_lo,
    halo,
    hot_x,
    hot_y,
    at_vents,
    from_adjoint,
    term,
    term_in,
    by_gy,
    by_gx,
    ld_sem,
    c0_send,
    c0_recv,
    lg_send,
    lg_recv,
    hx_send,
    hx_recv,
    pt_send,
    pt_recv,
    sn_send,
    sn_recv,
):
    nz, nr, nc = c0.shape
    n_chunks = nz // CHUNK
    n_direct = nz - N_LONG
    first_long = nz - 3 * N_LONG
    early_direct = first_long + 2 * EARLY_LONG
    s = lax.axis_index("section")
    gx = lax.axis_index("gx")
    gy = lax.axis_index("gy")
    ngx, ngy = lax.axis_size("gx"), lax.axis_size("gy")
    half = (nr, LANES)
    lane = lax.broadcasted_iota(jnp.int32, half, 1)
    row = lax.broadcasted_iota(jnp.int32, half, 0)
    halves = (slice(0, LANES), slice(LANES, 2 * LANES))

    partner = {"section": 1 - s}
    cross = {"section": 1 - s, "gx": gx + 1 - 2 * lax.rem(gx, 2)}
    beside = (
        {"gy": lax.rem(gy + 1, ngy)},
        {"gy": lax.rem(gy + ngy - 1, ngy)},
        {"gx": lax.rem(gx + 1, ngx)},
        {"gx": lax.rem(gx + ngx - 1, ngx)},
    )

    def remote(src, dst, send, recv, to):
        return pltpu.make_async_remote_copy(
            src, dst, send, recv, device_id=to, device_id_type=MESH
        )

    def loads(i):
        at = pl.ds(i * CHUNK, CHUNK)
        return (
            pltpu.make_async_copy(fields_ref.at[0, :, at], slots.at[:, at], ld_sem.at[0, i]),
            pltpu.make_async_copy(cx_ref.at[at], cx.at[at], ld_sem.at[1, i]),
            pltpu.make_async_copy(cy_ref.at[at], cy.at[at], ld_sem.at[2, i]),
        )

    def direct(z):
        return remote(c0.at[z], c0.at[z], c0_send.at[z], c0_recv.at[z], partner)

    def start_direct(i):
        over = jnp.maximum(i - first_long, 0)
        late = first_long + 1 + 3 * (over // 2) + lax.rem(over, 2)
        direct(jnp.where(i < first_long, i, late)).start()

    def long_plane(j):
        return first_long + 3 * j

    def long_one(j):
        z = long_plane(j)
        return remote(c0.at[z], long_buf.at[j], c0_send.at[z], lg_recv.at[j], cross)

    def long_two(j):
        return remote(long_buf.at[j], long_buf.at[j], lg_send.at[j], lg_recv.at[j], partner)

    def long_three(j):
        z = long_plane(j)
        return remote(long_buf.at[j], c0.at[z], lg_send.at[j], c0_recv.at[z], cross)

    def exchange(e):
        return (
            remote(pack_out.at[e], got_w.at[e], hx_send.at[e, 0], hx_recv.at[e, 0], beside[0]),
            remote(pack_out.at[e], got_e.at[e], hx_send.at[e, 1], hx_recv.at[e, 1], beside[1]),
            remote(edge_hi.at[e], got_xw.at[e], hx_send.at[e, 2], hx_recv.at[e, 2], beside[2]),
            remote(edge_lo.at[e], got_xe.at[e], hx_send.at[e, 3], hx_recv.at[e, 3], beside[3]),
        )

    def to_partner():
        return (
            remote(pack_out.at[1], part_p, pt_send.at[0], pt_recv.at[0], partner),
            remote(edge_hi.at[1], part_hi, pt_send.at[1], pt_recv.at[1], partner),
            remote(edge_lo.at[1], part_lo, pt_send.at[2], pt_recv.at[2], partner),
        )

    def spread(d):
        to = {"gy": lax.rem(gy + d, ngy)}
        return remote(term, by_gy.at[d - 1], sn_send.at[d - 1], sn_recv.at[d - 1], to)

    def spread_rows(d):
        to = {"gx": lax.rem(gx + d, ngx)}
        i = ngy - 1 + d - 1
        return remote(by_gy.at[ngy - 1], by_gx.at[d - 1], sn_send.at[i], sn_recv.at[i], to)

    def last_sums():
        i = ngy + ngx - 2
        return remote(by_gx.at[ngx - 1], by_gx.at[ngx - 1], sn_send.at[i], sn_recv.at[i], partner)

    def to_forward():
        i = ngy + ngx - 1
        return (
            remote(at_vents, from_adjoint, sn_send.at[i], sn_recv.at[i], partner),
            remote(term, term_in, sn_send.at[i + 1], sn_recv.at[i + 1], partner),
        )

    def prepare_vents():
        cells = where_ref[...]
        width = nc * ngy
        bits = width.bit_length() - 1
        assert width == 1 << bits
        rows = lax.shift_right_logical(cells, bits) - gx * nr
        cols = (cells & (width - 1)) - gy * nc
        hot_x[...] = (lax.broadcasted_iota(jnp.int32, hot_x.shape, 0) == rows).astype(jnp.float32)
        hot_y[...] = (lax.broadcasted_iota(jnp.int32, hot_y.shape, 0) == cols).astype(jnp.float32)

    def vents_of(values):
        found = jnp.dot(
            values.reshape(-1, nc),
            hot_y[...],
            precision=lax.Precision.HIGHEST,
            preferred_element_type=jnp.float32,
        )
        found = found.reshape(-1, nr, hot_x.shape[1]) * hot_x[...][None]
        return jnp.sum(found, 1)

    def gather_vents(ref, weighted):
        @pl.loop(0, nz // 8)
        def _(b):
            z = pl.multiple_of(b * 8, 8)
            found = vents_of(ref[pl.ds(z, 8)])
            if weighted:
                sub = lax.broadcasted_iota(jnp.int32, found.shape, 0)
                weight = jnp.full(found.shape, prof_ref[z], jnp.float32)
                for i in range(1, 8):
                    weight = jnp.where(sub == i, prof_ref[z + i], weight)
                found = found * weight
            at_vents[pl.ds(z, 8), :] = found

    def finish_exchange(e):
        for copy in exchange(e):
            copy.wait_recv()
        west = jnp.where(gy > 0, 1.0, 0.0)
        east = jnp.where(gy < ngy - 1, 1.0, 0.0)
        low = jnp.where(gx > 0, 1.0, 0.0)
        high = jnp.where(gx < ngx - 1, 1.0, 0.0)
        moved = pltpu.roll(got_e[e], LANES - 2, 1)
        halo[...] = jnp.where(lax.rem(lane, 2) == 0, got_w[e] * west, moved * east)
        got_xw[e] = got_xw[e] * low
        got_xe[e] = got_xe[e] * high

    def pack(ref, z, left, right, *at):
        both = pltpu.roll(jnp.where(lane == LANES - 1, right, left), 2 * z + 1, 1)
        where = (*at, slice(None), slice(None))
        ref[where] = jnp.where(lane // 2 == z, both, ref[where])

    def neighbours(z, e, f, gxs, gys):
        side = pltpu.roll(halo[...], lax.rem(2 * nz - 2 * z, LANES), 1)
        lo = [pltpu.roll(a, 1, 1) for a in f]
        hi = [pltpu.roll(a, LANES - 1, 1) for a in gys]
        south = (jnp.where(lane == 0, side, lo[0]), jnp.where(lane == 0, lo[0], lo[1]))
        north = (
            jnp.where(lane == LANES - 1, hi[1], hi[0]),
            jnp.where(lane == LANES - 1, side, hi[1]),
        )
        below = [got_xw[e, z, :, at] for at in halves]
        above = [got_xe[e, z, :, at] for at in halves]
        west = [jnp.where(row == 0, b, pltpu.roll(a, 1, 0)) for a, b in zip(f, below)]
        east = [jnp.where(row == nr - 1, b, pltpu.roll(a, nr - 1, 0)) for a, b in zip(gxs, above)]
        return west, east, south, north

    def read(ref, z):
        return [ref[z, :, at] for at in halves]

    def vertical(z):
        up, down = jnp.minimum(z + 1, nz - 1), jnp.maximum(z - 1, 0)
        return up, down, jnp.where(z < nz - 1, 1.0, 0.0), jnp.where(z > 0, 1.0, 0.0)

    def forward(src, z, e):
        f, u, v = read(src, z), read(cx, z), read(cy, z)
        h, k = h_ref[z], k_ref[z]
        if e is None:
            west = [pltpu.roll(a, 1, 0) for a in f]
            east = [pltpu.roll(a, nr - 1, 0) for a in f]
            lo = [pltpu.roll(a, 1, 1) for a in f]
            hi = [pltpu.roll(a, LANES - 1, 1) for a in f]
            south = (lo[0], jnp.where(lane == 0, lo[0], lo[1]))
            north = (jnp.where(lane == LANES - 1, hi[1], hi[0]), hi[1])
        else:
            west, east, south, north = neighbours(z, e, f, f, f)
        up, down, has_up, has_down = vertical(z)
        above, below = read(src, up), read(src, down)
        level = 1.0 - 4.0 * h - 2.0 * k
        out = []
        for i, at in enumerate(halves):
            total = (level - u[i] - v[i]) * f[i] + u[i] * west[i] + v[i] * south[i]
            total = total + h * ((west[i] + east[i]) + (south[i] + north[i]))
            total = total + (k * has_up) * above[i] + (k * has_down) * below[i]
            washed, _ = wash_and_slope(f[i])
            out.append(total - rate[:, at] * washed + prof_ref[z] * column[:, at])
        return out

    def transposed(src, z, e):
        f, u, v = read(src, z), read(cx, z), read(cy, z)
        h, k = h_ref[z], k_ref[z]
        qx = [(b + h) * a for a, b in zip(f, u)]
        qy = [(b + h) * a for a, b in zip(f, v)]
        west, east, south, north = neighbours(z, e, f, qx, qy)
        up, down, has_up, has_down = vertical(z)
        above, below = read(src, up), read(src, down)
        k_up, k_down = k_ref[up] * has_up, k_ref[down] * has_down
        level = 1.0 - 4.0 * h - 2.0 * k
        out = []
        for i in range(2):
            total = (level - u[i] - v[i]) * f[i] + east[i] + north[i] + h * (west[i] + south[i])
            out.append(total + k_up * above[i] + k_down * below[i])
        return out

    def selected(z):
        pick = jnp.full(half, pick_ref[s], jnp.int32)
        out = []
        for at in halves:
            a = jnp.where(pick == 0, slots[0, z, :, at], slots[1, z, :, at])
            b = jnp.where(pick == 2, slots[2, z, :, at], slots[3, z, :, at])
            out.append(jnp.where(pick < 2, a, b))
        return out

    def prepare_columns():
        kind = class_ref[...]
        value = jnp.full(kind.shape, rates_ref[0], jnp.float32)
        for c in range(1, rates_ref.shape[0]):
            value = jnp.where(kind == c, rates_ref[c], value)
        rate[...] = value
        column[...] = jnp.zeros_like(column)

        @pl.loop(0, cells_ref.shape[0])
        def _(v):
            column[...] += jnp.where(cell_ids() == cells_ref[v], vent_ref[v], 0.0)

    def cell_ids():
        rows = lax.broadcasted_iota(jnp.int32, (nr, nc), 0) + gx * nr
        return rows * (nc * ngy) + lax.broadcasted_iota(jnp.int32, (nr, nc), 1) + gy * nc

    @pl.loop(0, n_chunks)
    def _(i):
        for copy in loads(i):
            copy.start()

    barrier = pltpu.get_barrier_semaphore()
    along_gy = [{"gy": lax.rem(gy + d, ngy)} for d in range(1, ngy)]
    along_gx = [{"gx": lax.rem(gx + d, ngx)} for d in range(1, ngx)]
    peers = (partner, cross, *along_gy, *along_gx)
    for peer in peers:
        pl.semaphore_signal(barrier, 1, device_id=peer, device_id_type=MESH)
    pl.semaphore_wait(barrier, len(peers))

    @pl.when(s == 0)
    def _():
        def relay(j):
            long_two(j).wait_recv()
            long_three(j).start()

        @pl.loop(0, n_chunks)
        def _(i):
            for copy in loads(i):
                copy.wait()

            @pl.loop(0, CHUNK)
            def _(t):
                z = i * CHUNK + t
                f = selected(z)
                for at, value in zip(halves, f):
                    c0[z, :, at] = value
                    edge_hi[0, z, :, at] = value[nr - 1 : nr]
                    edge_lo[0, z, :, at] = value[0:1]
                pack(pack_out, z, f[0], f[1], 0)
                place = z - first_long
                is_long = (place >= 0) & (lax.rem(place + 3 * nz, 3) == 0)
                now = z < first_long + 3 * EARLY_LONG

                @pl.when(now & is_long)
                def _():
                    long_one((place + 3 * nz) // 3 - nz).start()

                @pl.when(now & jnp.logical_not(is_long))
                def _():
                    direct(z).start()

        for copy in exchange(0):
            copy.start()
        prepare_columns()
        finish_exchange(0)

        @pl.loop(0, nz)
        def _(z):
            new = forward(c0, z, 0)
            for at, value in zip(halves, new):
                state[z, :, at] = value
                edge_hi[1, z, :, at] = value[nr - 1 : nr]
                edge_lo[1, z, :, at] = value[0:1]
            pack(pack_out, z, new[0], new[1], 1)

            @pl.when(lax.rem(z, 8) == 7)
            def _():
                start_direct(early_direct + z // 8)
                long_one(EARLY_LONG + z // 8).start()

            @pl.when(lax.rem(z, 16) == 15)
            def _():
                relay(z // 16)

        for copy in (*to_partner(), *exchange(1)):
            copy.start()
        prepare_vents()
        gather_vents(state, False)
        finish_exchange(1)

        @pl.loop(0, nz)
        def _(z):
            new = forward(state, z, 1)
            for at, value in zip(halves, new):
                out_ref[z, :, at] = value

            @pl.when(lax.rem(z, 8) == 3)
            def _():
                start_direct(early_direct + nz // 8 + z // 8)
                long_one(EARLY_LONG + nz // 8 + z // 8).start()

            @pl.when(lax.rem(z, 16) == 15)
            def _():
                relay(nz // 16 + z // 16)

        for j in range(EARLY_LONG + nz // 4, N_LONG):
            long_one(j).start()
        for i in range(4):
            start_direct(early_direct + nz // 4 + i)

        for copy in to_forward():
            copy.wait_recv()
        _, slope = wash_and_slope(at_vents[...])
        lost = jnp.sum(slope * from_adjoint[...], 0, keepdims=True) * vents_of(rate[...])
        term[...] = term_in[...] - lost
        for d in range(1, ngy):
            spread(d).start()
        relay(nz // 8)
        total = term[...]
        for d in range(1, ngy):
            spread(d).wait_recv()
            total = total + by_gy[d - 1]
        by_gy[ngy - 1] = total
        for d in range(1, ngx):
            spread_rows(d).start()
        relay(nz // 8 + 1)
        for d in range(1, ngx):
            spread_rows(d).wait_recv()
            total = total + by_gx[d - 1]
        by_gx[ngx - 1] = total
        last_sums().start()

        @pl.loop(0, N_LONG - nz // 8 - 2)
        def _(k):
            for t in range(2):
                i = early_direct + nz // 4 + 4 + 2 * k + t

                @pl.when(i < n_direct)
                def _():
                    start_direct(i)

            relay(nz // 8 + 2 + k)

        sums_ref[...] = total

        @pl.loop(0, N_LONG)
        def _(j):
            long_three(j).wait_send()

        @pl.loop(0, nz)
        def _(z):
            direct(z).wait_send()

        for copy in (*to_partner(), *exchange(0), *exchange(1), last_sums()):
            copy.wait_send()
        for d in range(1, ngy):
            spread(d).wait_send()
        for d in range(1, ngx):
            spread_rows(d).wait_send()

    @pl.when(s == 1)
    def _():
        def relay(j):
            long_one(j).wait_recv()
            long_two(j).start()

        @pl.loop(0, n_chunks)
        def _(i):
            for copy in loads(i):
                copy.wait()

            @pl.loop(0, CHUNK)
            def _(t):
                z = i * CHUNK + t
                f = selected(z)
                h = h_ref[z]
                for at, value in zip(halves, f):
                    lam2[z, :, at] = value
                    first = value[0:1]
                    coef = cx[z, 0:1, at] + h
                    edge_hi[0, z, :, at] = value[nr - 1 : nr]
                    edge_lo[0, z, :, at] = coef * first
                    edge_f0[z, :, at] = first
                    edge_c0[z, :, at] = coef
                pack(pack_f, z, f[0], f[1])
                pack(pack_c, z, cy[z, :, 0:LANES] + h, jnp.ones(half, jnp.float32))

        pack_out[0] = pack_f[...] * pack_c[...]
        for copy in exchange(0):
            copy.start()
        for j in range(EARLY_LONG):
            relay(j)
        prepare_columns()
        prepare_vents()
        colsum[...] = jnp.zeros_like(colsum)
        finish_exchange(0)

        @pl.loop(0, nz)
        def _(z):
            new = transposed(lam2, z, 0)
            for at, value in zip(halves, new):
                state[z, :, at] = value
                colsum[:, at] += prof_ref[z] * (value + lam2[z, :, at])
                edge_mhi[z, :, at] = value[nr - 1 : nr]
                edge_mlo[z, :, at] = value[0:1]
            pack(pack_m, z, new[0], new[1])

            @pl.when(lax.rem(z, 8) == 7)
            def _():
                relay(z // 8 + EARLY_LONG)

        gather_vents(lam2, True)
        term[...] = vents_of(colsum[...])
        for copy in to_forward():
            copy.start()
        for copy in to_partner():
            copy.wait_recv()
        _, slope = wash_and_slope(part_hi[...])
        edge_hi[1] = edge_mhi[...] - rate[nr - 1 : nr, :] * slope * edge_hi[0]
        _, slope = wash_and_slope(part_lo[...])
        edge_mlo[...] = edge_mlo[...] - rate[0:1, :] * slope * edge_f0[...]
        edge_lo[1] = edge_mlo[...] * edge_c0[...]
        side_rate = jnp.where(
            lax.rem(lane, 2) == 0,
            jnp.broadcast_to(rate[:, nc - 1 : nc], half),
            jnp.broadcast_to(rate[:, 0:1], half),
        )
        _, slope = wash_and_slope(part_p[...])
        pack_m[...] = pack_m[...] - side_rate * slope * pack_f[...]
        pack_out[1] = pack_m[...] * pack_c[...]
        for copy in exchange(1):
            copy.start()
        finish_exchange(1)

        def last(z):
            lam = read(state, z)
            new = transposed(state, z, 1)
            conc = read(c0, z)
            for i, at in enumerate(halves):
                _, bend = wash_and_slope(conc[i])
                out_ref[z, :, at] = new[i] - rate[:, at] * bend * lam[i]

        direct(0).wait_recv()

        @pl.loop(0, nz)
        def _(z):
            @pl.when((lax.rem(z, 3) == 0) & (z // 3 < N_LONG - EARLY_LONG - nz // 8))
            def _():
                relay(EARLY_LONG + nz // 8 + z // 3)

            @pl.when(z < nz - 1)
            def _():
                direct(z + 1).wait_recv()

            conc = forward(c0, z, None)
            old, field = read(state, z), read(lam2, z)
            sides = pltpu.roll(pack_m[...], lax.rem(2 * nz - 2 * z + LANES - 1, LANES), 1)
            keep = (lane == 0, lane == LANES - 1)
            for i, at in enumerate(halves):
                _, bend = wash_and_slope(conc[i])
                lam = old[i] - rate[:, at] * bend * field[i]
                lam = jnp.where(keep[i], sides, lam)
                lam = jnp.where(row == 0, edge_mlo[z, :, at], lam)
                lam = jnp.where(row == nr - 1, edge_hi[1, z, :, at], lam)
                state[z, :, at] = lam

            @pl.when(z > 0)
            def _():
                last(z - 1)

        last(nz - 1)

        last_sums().wait_recv()
        sums_ref[...] = by_gx[ngx - 1]

        @pl.loop(0, N_LONG)
        def _(j):
            long_two(j).wait_send()

        for copy in (*exchange(0), *exchange(1), *to_forward()):
            copy.wait_send()


def shards(
    fields,
    slot_pick,
    courant_x,
    courant_y,
    horiz_diff,
    vert_diff,
    precip_class,
    class_rates,
    vent_cells,
    vent_rate,
    profile,
):
    nz, nr, nc = courant_x.shape
    vents = vent_cells.shape[0]
    ngx, ngy = lax.axis_size("gx"), lax.axis_size("gy")
    anywhere = pl.BlockSpec(memory_space=pl.ANY)
    scalars = pl.BlockSpec(memory_space=pltpu.SMEM)
    vector = pl.BlockSpec(memory_space=pltpu.VMEM)
    f32 = jnp.float32
    plane = pltpu.VMEM((nz, nr, nc), f32)
    tile = pltpu.VMEM((nr, nc), f32)
    packed = pltpu.VMEM((nr, LANES), f32)
    edge = pltpu.VMEM((nz, 1, nc), f32)
    packed2 = pltpu.VMEM((2, nr, LANES), f32)
    edge2 = pltpu.VMEM((2, nz, 1, nc), f32)
    dma = pltpu.SemaphoreType.DMA
    window, sums = pl.pallas_call(
        kernel,
        out_shape=(
            pltpu.VMEM((nz, nr, nc), f32),
            jax.ShapeDtypeStruct((1, vents), f32),
        ),
        in_specs=[anywhere] * 3 + [scalars] * 7 + [vector] * 2,
        out_specs=(vector, vector),
        scratch_shapes=[
            pltpu.VMEM((fields.shape[1], nz, nr, nc), f32),
            plane,
            plane,
            plane,
            plane,
            plane,
            pltpu.VMEM((N_LONG, nr, nc), f32),
            tile,
            tile,
            tile,
            packed,
            packed,
            packed,
            packed2,
            edge2,
            edge2,
            edge,
            edge,
            edge,
            edge,
            packed2,
            packed2,
            edge2,
            edge2,
            packed,
            edge,
            edge,
            packed,
            pltpu.VMEM((nr, vents), f32),
            pltpu.VMEM((nc, vents), f32),
            pltpu.VMEM((nz, vents), f32),
            pltpu.VMEM((nz, vents), f32),
            pltpu.VMEM((1, vents), f32),
            pltpu.VMEM((1, vents), f32),
            pltpu.VMEM((ngy, 1, vents), f32),
            pltpu.VMEM((ngx, 1, vents), f32),
            dma((3, nz // CHUNK)),
            dma((nz,)),
            dma((nz,)),
            dma((N_LONG,)),
            dma((N_LONG,)),
            dma((2, 4)),
            dma((2, 4)),
            dma((3,)),
            dma((3,)),
            dma((ngy + ngx + 1,)),
            dma((ngy + ngx + 1,)),
        ],
        compiler_params=pltpu.CompilerParams(
            collective_id=0, has_side_effects=True, vmem_limit_bytes=58 << 20
        ),
    )(
        fields,
        courant_x,
        courant_y,
        slot_pick,
        horiz_diff,
        vert_diff,
        class_rates,
        vent_cells,
        vent_rate,
        profile,
        precip_class,
        vent_cells.reshape(1, vents),
    )
    return window[None], sums.reshape(vents)


def solution(mesh):
    placed = (
        P("section", None, None, "gx", "gy"),
        P(),
        P(None, "gx", "gy"),
        P(None, "gx", "gy"),
        P(),
        P(),
        P("gx", "gy"),
        P(),
        P(),
        P(),
        P(),
    )
    return jax.shard_map(
        shards,
        mesh=mesh,
        in_specs=placed,
        out_specs=(P("section", None, "gx", "gy"), P()),
        check_vma=False,
    )
```

```python
import jax
import jax.numpy as jnp
from jax import lax
from jax.experimental import pallas as pl
from jax.experimental.pallas import tpu as pltpu
from jax.sharding import PartitionSpec as P

MESH = pl.DeviceIdType.MESH
LANES = 128
CHUNK = 4
GROUPS = 8
SKIP = 2
N_LONG = 3 * GROUPS - SKIP
EARLY = 16
EARLY_ROUNDS = 10
EVERY = 8


def wash_and_slope(conc):
    square = conc * conc
    inverse = 1.0 / (1.0 + square)
    return square * inverse, 2.0 * conc * inverse * inverse


def kernel(
    fields_ref,
    cx_ref,
    cy_ref,
    pick_ref,
    h_ref,
    k_ref,
    rates_ref,
    cells_ref,
    vent_ref,
    prof_ref,
    class_ref,
    where_ref,
    out_ref,
    sums_ref,
    slots,
    c0,
    lam2,
    cx,
    cy,
    state,
    long_buf,
    rate,
    column,
    colsum,
    pack_f,
    pack_c,
    pack_m,
    pack_out,
    edge_hi,
    edge_lo,
    edge_f0,
    edge_c0,
    edge_mhi,
    edge_mlo,
    got_w,
    got_e,
    got_xw,
    got_xe,
    part_p,
    part_hi,
    part_lo,
    halo,
    rows_hi,
    rows_lo,
    hot_x,
    hot_y,
    at_vents,
    from_adjoint,
    term,
    term_in,
    by_gy,
    by_gx,
    ld_sem,
    rw_sem,
    c0_send,
    c0_recv,
    lg_send,
    lg_recv,
    hx_send,
    hx_recv,
    pt_send,
    pt_recv,
    sn_send,
    sn_recv,
):
    nz, nr, nc = c0.shape
    n_chunks = nz // CHUNK
    n_direct = nz - N_LONG
    first_long = 8 * (SKIP // 3) + (1, 4, 6)[SKIP % 3]
    early_direct = EARLY - max(3 * (EARLY // 8) - SKIP, 0)
    s = lax.axis_index("section")
    gx = lax.axis_index("gx")
    gy = lax.axis_index("gy")
    ngx, ngy = lax.axis_size("gx"), lax.axis_size("gy")
    half = (nr, LANES)
    lane = lax.broadcasted_iota(jnp.int32, half, 1)
    row = lax.broadcasted_iota(jnp.int32, half, 0)
    halves = (slice(0, LANES), slice(LANES, 2 * LANES))

    partner = {"section": 1 - s}
    cross = {"section": 1 - s, "gx": gx + 1 - 2 * lax.rem(gx, 2)}
    aside = (
        {"section": 1 - s, "gx": lax.rem(gx + 1, ngx)},
        {"section": 1 - s, "gx": lax.rem(gx + ngx - 1, ngx)},
    )
    beside = (
        {"gy": lax.rem(gy + 1, ngy)},
        {"gy": lax.rem(gy + ngy - 1, ngy)},
        {"gx": lax.rem(gx + 1, ngx)},
        {"gx": lax.rem(gx + ngx - 1, ngx)},
    )

    def remote(src, dst, send, recv, to):
        return pltpu.make_async_remote_copy(
            src, dst, send, recv, device_id=to, device_id_type=MESH
        )

    def chunk(i):
        lead = first_long // CHUNK
        return jnp.where(i == 0, lead, jnp.where(i <= lead, i - 1, i))

    def loads(i):
        at = pl.ds(chunk(i) * CHUNK, CHUNK)
        return (
            pltpu.make_async_copy(fields_ref.at[0, :, at], slots.at[:, at], ld_sem.at[0, i]),
            pltpu.make_async_copy(cx_ref.at[at], cx.at[at], ld_sem.at[1, i]),
            pltpu.make_async_copy(cy_ref.at[at], cy.at[at], ld_sem.at[2, i]),
        )

    def row_loads():
        high, low = pl.ds(nr - 1, 1), pl.ds(0, 1)
        return (
            pltpu.make_async_copy(fields_ref.at[0, :, :, high], rows_hi, rw_sem.at[0]),
            pltpu.make_async_copy(fields_ref.at[0, :, :, low], rows_lo, rw_sem.at[1]),
            pltpu.make_async_copy(cx_ref.at[:, low], edge_c0, rw_sem.at[2]),
        )

    def selected_rows(ref):
        pick = jnp.full(ref.shape[1:], pick_ref[s], jnp.int32)
        a = jnp.where(pick == 0, ref[0], ref[1])
        b = jnp.where(pick == 2, ref[2], ref[3])
        return jnp.where(pick < 2, a, b)

    def direct(z):
        return remote(c0.at[z], c0.at[z], c0_send.at[z], c0_recv.at[z], partner)

    def start_direct(i):
        late = jnp.maximum(i - SKIP, 0)
        r = lax.rem(late, 5)
        paired = 8 * (late // 5) + r + (r + 3) // 4 + r // 3 + r // 4
        direct(jnp.where(i < first_long, i, paired)).start()

    def long_plane(j):
        r = lax.rem(j + SKIP, 3)
        return 8 * ((j + SKIP) // 3) + 1 + 3 * r - r // 2

    def long_one(j):
        z = long_plane(j)
        return remote(c0.at[z], long_buf.at[j], c0_send.at[z], lg_recv.at[j], cross)

    def long_two(j):
        return remote(long_buf.at[j], long_buf.at[j], lg_send.at[j], lg_recv.at[j], partner)

    def long_three(j):
        z = long_plane(j)
        return remote(long_buf.at[j], c0.at[z], lg_send.at[j], c0_recv.at[z], cross)

    def exchange(e):
        return (
            remote(pack_out.at[e], got_w.at[e], hx_send.at[e, 0], hx_recv.at[e, 0], beside[0]),
            remote(pack_out.at[e], got_e.at[e], hx_send.at[e, 1], hx_recv.at[e, 1], beside[1]),
            remote(edge_hi.at[e], got_xw.at[e], hx_send.at[e, 2], hx_recv.at[e, 2], beside[2]),
            remote(edge_lo.at[e], got_xe.at[e], hx_send.at[e, 3], hx_recv.at[e, 3], beside[3]),
        )

    def onward():
        return (
            remote(part_hi, got_xw.at[1], pt_send.at[1], hx_recv.at[1, 2], aside[0]),
            remote(part_lo, got_xe.at[1], pt_send.at[2], hx_recv.at[1, 3], aside[1]),
        )

    def to_partner():
        return (
            remote(pack_out.at[1], part_p, pt_send.at[0], pt_recv.at[0], partner),
            remote(edge_hi.at[1], part_hi, pt_send.at[1], pt_recv.at[1], partner),
            remote(edge_lo.at[1], part_lo, pt_send.at[2], pt_recv.at[2], partner),
        )

    def spread(d):
        to = {"gy": lax.rem(gy + d, ngy)}
        return remote(term, by_gy.at[d - 1], sn_send.at[d - 1], sn_recv.at[d - 1], to)

    def spread_rows(d):
        to = {"gx": lax.rem(gx + d, ngx)}
        i = ngy - 1 + d - 1
        return remote(by_gy.at[ngy - 1], by_gx.at[d - 1], sn_send.at[i], sn_recv.at[i], to)

    def last_sums():
        i = ngy + ngx - 2
        return remote(by_gx.at[ngx - 1], by_gx.at[ngx - 1], sn_send.at[i], sn_recv.at[i], partner)

    def to_forward():
        i = ngy + ngx - 1
        return (
            remote(at_vents, from_adjoint, sn_send.at[i], sn_recv.at[i], partner),
            remote(term, term_in, sn_send.at[i + 1], sn_recv.at[i + 1], partner),
        )

    def prepare_vents():
        cells = where_ref[...]
        width = nc * ngy
        bits = width.bit_length() - 1
        assert width == 1 << bits
        rows = lax.shift_right_logical(cells, bits) - gx * nr
        cols = (cells & (width - 1)) - gy * nc
        hot_x[...] = (lax.broadcasted_iota(jnp.int32, hot_x.shape, 0) == rows).astype(jnp.float32)
        hot_y[...] = (lax.broadcasted_iota(jnp.int32, hot_y.shape, 0) == cols).astype(jnp.float32)

    def vents_of(values):
        found = jnp.dot(
            values.reshape(-1, nc),
            hot_y[...],
            precision=lax.Precision.HIGHEST,
            preferred_element_type=jnp.float32,
        )
        found = found.reshape(-1, nr, hot_x.shape[1]) * hot_x[...][None]
        return jnp.sum(found, 1)

    def gather_vents(ref, weighted, every_other=None):
        @pl.loop(0, nz // 8)
        def _(b):
            z = pl.multiple_of(b * 8, 8)
            found = vents_of(ref[pl.ds(z, 8)])
            if weighted:
                sub = lax.broadcasted_iota(jnp.int32, found.shape, 0)
                weight = jnp.full(found.shape, prof_ref[z], jnp.float32)
                for i in range(1, 8):
                    weight = jnp.where(sub == i, prof_ref[z + i], weight)
                found = found * weight
            at_vents[pl.ds(z, 8), :] = found
            if every_other:
                pl.when(lax.rem(b, 2) == 1)(lambda: every_other(b))

    def finish_exchange(e):
        for copy in exchange(e):
            copy.wait_recv()
        west = jnp.where(gy > 0, 1.0, 0.0)
        east = jnp.where(gy < ngy - 1, 1.0, 0.0)
        low = jnp.where(gx > 0, 1.0, 0.0)
        high = jnp.where(gx < ngx - 1, 1.0, 0.0)
        moved = pltpu.roll(got_e[e], LANES - 2, 1)
        halo[...] = jnp.where(lax.rem(lane, 2) == 0, got_w[e] * west, moved * east)
        got_xw[e] = got_xw[e] * low
        got_xe[e] = got_xe[e] * high

    def pack(ref, z, left, right, *at):
        both = pltpu.roll(jnp.where(lane == LANES - 1, right, left), 2 * z + 1, 1)
        where = (*at, slice(None), slice(None))
        ref[where] = jnp.where(lane // 2 == z, both, ref[where])

    def neighbours(z, e, f, gxs, gys):
        side = pltpu.roll(halo[...], lax.rem(2 * nz - 2 * z, LANES), 1)
        lo = [pltpu.roll(a, 1, 1) for a in f]
        hi = [pltpu.roll(a, LANES - 1, 1) for a in gys]
        south = (jnp.where(lane == 0, side, lo[0]), jnp.where(lane == 0, lo[0], lo[1]))
        north = (
            jnp.where(lane == LANES - 1, hi[1], hi[0]),
            jnp.where(lane == LANES - 1, side, hi[1]),
        )
        below = [got_xw[e, z, :, at] for at in halves]
        above = [got_xe[e, z, :, at] for at in halves]
        west = [jnp.where(row == 0, b, pltpu.roll(a, 1, 0)) for a, b in zip(f, below)]
        east = [jnp.where(row == nr - 1, b, pltpu.roll(a, nr - 1, 0)) for a, b in zip(gxs, above)]
        return west, east, south, north

    def read(ref, z):
        return [ref[z, :, at] for at in halves]

    def vertical(z):
        up, down = jnp.minimum(z + 1, nz - 1), jnp.maximum(z - 1, 0)
        return up, down, jnp.where(z < nz - 1, 1.0, 0.0), jnp.where(z > 0, 1.0, 0.0)

    def forward(src, z, e):
        f, u, v = read(src, z), read(cx, z), read(cy, z)
        h, k = h_ref[z], k_ref[z]
        if e is None:
            west = [pltpu.roll(a, 1, 0) for a in f]
            east = [pltpu.roll(a, nr - 1, 0) for a in f]
            lo = [pltpu.roll(a, 1, 1) for a in f]
            hi = [pltpu.roll(a, LANES - 1, 1) for a in f]
            south = (lo[0], jnp.where(lane == 0, lo[0], lo[1]))
            north = (jnp.where(lane == LANES - 1, hi[1], hi[0]), hi[1])
        else:
            west, east, south, north = neighbours(z, e, f, f, f)
        up, down, has_up, has_down = vertical(z)
        above, below = read(src, up), read(src, down)
        level = 1.0 - 4.0 * h - 2.0 * k
        out = []
        for i, at in enumerate(halves):
            total = (level - u[i] - v[i]) * f[i] + u[i] * west[i] + v[i] * south[i]
            total = total + h * ((west[i] + east[i]) + (south[i] + north[i]))
            total = total + (k * has_up) * above[i] + (k * has_down) * below[i]
            washed, _ = wash_and_slope(f[i])
            out.append(total - rate[:, at] * washed + prof_ref[z] * column[:, at])
        return out

    def transposed(src, z, e):
        f, u, v = read(src, z), read(cx, z), read(cy, z)
        h, k = h_ref[z], k_ref[z]
        qx = [(b + h) * a for a, b in zip(f, u)]
        qy = [(b + h) * a for a, b in zip(f, v)]
        west, east, south, north = neighbours(z, e, f, qx, qy)
        up, down, has_up, has_down = vertical(z)
        above, below = read(src, up), read(src, down)
        k_up, k_down = k_ref[up] * has_up, k_ref[down] * has_down
        level = 1.0 - 4.0 * h - 2.0 * k
        out = []
        for i in range(2):
            total = (level - u[i] - v[i]) * f[i] + east[i] + north[i] + h * (west[i] + south[i])
            out.append(total + k_up * above[i] + k_down * below[i])
        return out

    def selected(z):
        pick = jnp.full(half, pick_ref[s], jnp.int32)
        out = []
        for at in halves:
            a = jnp.where(pick == 0, slots[0, z, :, at], slots[1, z, :, at])
            b = jnp.where(pick == 2, slots[2, z, :, at], slots[3, z, :, at])
            out.append(jnp.where(pick < 2, a, b))
        return out

    def prepare_columns():
        kind = class_ref[...]
        value = jnp.full(kind.shape, rates_ref[0], jnp.float32)
        for c in range(1, rates_ref.shape[0]):
            value = jnp.where(kind == c, rates_ref[c], value)
        rate[...] = value
        column[...] = jnp.zeros_like(column)

        @pl.loop(0, cells_ref.shape[0])
        def _(v):
            column[...] += jnp.where(cell_ids() == cells_ref[v], vent_ref[v], 0.0)

    def cell_ids():
        rows = lax.broadcasted_iota(jnp.int32, (nr, nc), 0) + gx * nr
        return rows * (nc * ngy) + lax.broadcasted_iota(jnp.int32, (nr, nc), 1) + gy * nc

    for copy in (loads(0)[0], *row_loads()):
        copy.start()
    for copy in loads(0)[1:]:
        copy.start()

    @pl.loop(1, n_chunks)
    def _(i):
        for copy in loads(i):
            copy.start()

    barrier = pltpu.get_barrier_semaphore()
    along_gy = [{"gy": lax.rem(gy + d, ngy)} for d in range(1, ngy)]
    along_gx = [{"gx": lax.rem(gx + d, ngx)} for d in range(1, ngx)]
    peers = (partner, *aside, *along_gy, *along_gx)
    for peer in peers:
        pl.semaphore_signal(barrier, 1, device_id=peer, device_id_type=MESH)
    pl.semaphore_wait(barrier, len(peers))

    def send_chunk(i):
        @pl.loop(0, CHUNK)
        def _(t):
            z = chunk(i) * CHUNK + t
            f = selected(z)
            for at, value in zip(halves, f):
                c0[z, :, at] = value
            pack(pack_out, z, f[0], f[1], 0)
            m = lax.rem(z, 8)
            is_long = (z >= first_long) & ((m == 1) | (m == 4) | (m == 6))

            @pl.when(is_long)
            def _():
                long_one(3 * (z // 8) + m // 4 + m // 6 - SKIP).start()

            @pl.when((z < EARLY) & jnp.logical_not(is_long))
            def _():
                direct(z).start()

    @pl.when(s == 0)
    def _():
        loads(0)[0].wait()
        send_chunk(0)

    for copy in row_loads():
        copy.wait()
    edge_hi[0] = selected_rows(rows_hi)
    edge_f0[...] = selected_rows(rows_lo)

    @pl.when(s == 0)
    def _():
        edge_lo[0] = edge_f0[...]

    @pl.when(s == 1)
    def _():
        @pl.loop(0, nz)
        def _(z):
            edge_c0[z] = edge_c0[z] + h_ref[z]

        edge_lo[0] = edge_c0[...] * edge_f0[...]

    for copy in exchange(0)[2:]:
        copy.start()

    @pl.when(s == 0)
    def _():
        def relay(j):
            long_two(j).wait_recv()
            long_three(j).start()

        def round_of(k):
            for t in range(2):
                i = early_direct + nz // 16 + 2 * k + t

                @pl.when(i < n_direct)
                def _():
                    start_direct(i)

            @pl.when(nz // 16 + k < N_LONG)
            def _():
                relay(nz // 16 + k)

        def pump_from(first, last):
            @pl.loop(first, last)
            def _(k):
                round_of(k)

        def pump(last):
            pump_from(0, last)

        @pl.loop(1, n_chunks)
        def _(i):
            for copy in loads(i):
                copy.wait()
            send_chunk(i)

        for copy in exchange(0)[:2]:
            copy.start()
        for copy in loads(0)[1:]:
            copy.wait()
        prepare_columns()
        finish_exchange(0)

        @pl.loop(0, nz)
        def _(z):
            new = forward(c0, z, 0)
            for at, value in zip(halves, new):
                state[z, :, at] = value
                edge_hi[1, z, :, at] = value[nr - 1 : nr]
                edge_lo[1, z, :, at] = value[0:1]
            pack(pack_out, z, new[0], new[1], 1)

            @pl.when(lax.rem(z, 16) == 7)
            def _():
                start_direct(early_direct + z // 16)

            @pl.when(lax.rem(z, 16) == 15)
            def _():
                relay(z // 16)

        for copy in (*to_partner(), *exchange(1)[:2]):
            copy.start()
        prepare_vents()
        gather_vents(state, False)
        pump(EARLY_ROUNDS)
        finish_exchange(1)

        @pl.loop(0, nz)
        def _(z):
            new = forward(state, z, 1)
            for at, value in zip(halves, new):
                out_ref[z, :, at] = value

            @pl.when(lax.rem(z, EVERY) == EVERY - 1)
            def _():
                round_of(EARLY_ROUNDS + z // EVERY)

        pump_from(EARLY_ROUNDS + nz // EVERY, N_LONG)
        for copy in to_forward():
            copy.wait_recv()
        _, slope = wash_and_slope(at_vents[...])
        lost = jnp.sum(slope * from_adjoint[...], 0, keepdims=True) * vents_of(rate[...])
        term[...] = term_in[...] - lost
        for d in range(1, ngy):
            spread(d).start()
        total = term[...]
        for d in range(1, ngy):
            spread(d).wait_recv()
            total = total + by_gy[d - 1]
        by_gy[ngy - 1] = total
        for d in range(1, ngx):
            spread_rows(d).start()
        for d in range(1, ngx):
            spread_rows(d).wait_recv()
            total = total + by_gx[d - 1]
        by_gx[ngx - 1] = total
        last_sums().start()
        sums_ref[...] = total

        @pl.loop(0, N_LONG)
        def _(j):
            long_three(j).wait_send()

        @pl.loop(0, nz)
        def _(z):
            direct(z).wait_send()

        for copy in (*to_partner(), *exchange(0), *exchange(1)[:2], last_sums()):
            copy.wait_send()
        for d in range(1, ngy):
            spread(d).wait_send()
        for d in range(1, ngx):
            spread_rows(d).wait_send()

    @pl.when(s == 1)
    def _():
        def relay(j):
            long_one(j).wait_recv()
            long_two(j).start()

        @pl.loop(0, n_chunks)
        def _(i):
            for copy in loads(i):
                copy.wait()

            @pl.loop(0, CHUNK)
            def _(t):
                z = chunk(i) * CHUNK + t
                f = selected(z)
                h = h_ref[z]
                for at, value in zip(halves, f):
                    lam2[z, :, at] = value
                pack(pack_f, z, f[0], f[1])
                pack(pack_c, z, cy[z, :, 0:LANES] + h, jnp.ones(half, jnp.float32))

        pack_out[0] = pack_f[...] * pack_c[...]
        for copy in exchange(0)[:2]:
            copy.start()
        prepare_columns()
        prepare_vents()
        colsum[...] = jnp.zeros_like(colsum)
        finish_exchange(0)

        @pl.loop(0, nz)
        def _(z):
            new = transposed(lam2, z, 0)
            for at, value in zip(halves, new):
                state[z, :, at] = value
                colsum[:, at] += prof_ref[z] * (value + lam2[z, :, at])
                edge_mhi[z, :, at] = value[nr - 1 : nr]
                edge_mlo[z, :, at] = value[0:1]
            pack(pack_m, z, new[0], new[1])

            @pl.when(lax.rem(z, 5) == 4)
            def _():
                relay(z // 5)

        gather_vents(lam2, True, lambda b: relay(12 + b // 2))
        term[...] = vents_of(colsum[...])
        for copy in to_forward():
            copy.start()
        for copy in to_partner():
            copy.wait_recv()
        for copy in onward():
            copy.start()
        _, slope = wash_and_slope(part_hi[...])
        edge_hi[1] = edge_mhi[...] - rate[nr - 1 : nr, :] * slope * edge_hi[0]
        _, slope = wash_and_slope(part_lo[...])
        edge_mlo[...] = edge_mlo[...] - rate[0:1, :] * slope * edge_f0[...]
        edge_lo[1] = edge_mlo[...] * edge_c0[...]
        side_rate = jnp.where(
            lax.rem(lane, 2) == 0,
            jnp.broadcast_to(rate[:, nc - 1 : nc], half),
            jnp.broadcast_to(rate[:, 0:1], half),
        )
        _, slope = wash_and_slope(part_p[...])
        pack_m[...] = pack_m[...] - side_rate * slope * pack_f[...]
        pack_out[1] = pack_m[...] * pack_c[...]
        for copy in exchange(1):
            copy.start()
        for j in range(16, 20):
            relay(j)
        finish_exchange(1)

        def last(z):
            lam = read(state, z)
            new = transposed(state, z, 1)
            conc = read(c0, z)
            for i, at in enumerate(halves):
                _, bend = wash_and_slope(conc[i])
                out_ref[z, :, at] = new[i] - rate[:, at] * bend * lam[i]

        direct(0).wait_recv()

        @pl.loop(0, nz)
        def _(z):
            @pl.when((lax.rem(z, 2) == 0) & (z // 2 < N_LONG - 20))
            def _():
                relay(20 + z // 2)

            @pl.when(z < nz - 1)
            def _():
                direct(z + 1).wait_recv()

            conc = forward(c0, z, None)
            old, field = read(state, z), read(lam2, z)
            sides = pltpu.roll(pack_m[...], lax.rem(2 * nz - 2 * z + LANES - 1, LANES), 1)
            keep = (lane == 0, lane == LANES - 1)
            for i, at in enumerate(halves):
                _, bend = wash_and_slope(conc[i])
                lam = old[i] - rate[:, at] * bend * field[i]
                lam = jnp.where(keep[i], sides, lam)
                lam = jnp.where(row == 0, edge_mlo[z, :, at], lam)
                lam = jnp.where(row == nr - 1, edge_hi[1, z, :, at], lam)
                state[z, :, at] = lam

            @pl.when(z > 0)
            def _():
                last(z - 1)

        last(nz - 1)

        last_sums().wait_recv()
        sums_ref[...] = by_gx[ngx - 1]

        @pl.loop(0, N_LONG)
        def _(j):
            long_two(j).wait_send()

        for copy in (*exchange(0), *exchange(1), *onward(), *to_forward()):
            copy.wait_send()


def shards(
    fields,
    slot_pick,
    courant_x,
    courant_y,
    horiz_diff,
    vert_diff,
    precip_class,
    class_rates,
    vent_cells,
    vent_rate,
    profile,
):
    nz, nr, nc = courant_x.shape
    vents = vent_cells.shape[0]
    ngx, ngy = lax.axis_size("gx"), lax.axis_size("gy")
    anywhere = pl.BlockSpec(memory_space=pl.ANY)
    scalars = pl.BlockSpec(memory_space=pltpu.SMEM)
    vector = pl.BlockSpec(memory_space=pltpu.VMEM)
    f32 = jnp.float32
    plane = pltpu.VMEM((nz, nr, nc), f32)
    tile = pltpu.VMEM((nr, nc), f32)
    packed = pltpu.VMEM((nr, LANES), f32)
    edge = pltpu.VMEM((nz, 1, nc), f32)
    packed2 = pltpu.VMEM((2, nr, LANES), f32)
    edge2 = pltpu.VMEM((2, nz, 1, nc), f32)
    dma = pltpu.SemaphoreType.DMA
    window, sums = pl.pallas_call(
        kernel,
        out_shape=(
            pltpu.VMEM((nz, nr, nc), f32),
            jax.ShapeDtypeStruct((1, vents), f32),
        ),
        in_specs=[anywhere] * 3 + [scalars] * 7 + [vector] * 2,
        out_specs=(vector, vector),
        scratch_shapes=[
            pltpu.VMEM((fields.shape[1], nz, nr, nc), f32),
            plane,
            plane,
            plane,
            plane,
            plane,
            pltpu.VMEM((N_LONG, nr, nc), f32),
            tile,
            tile,
            tile,
            packed,
            packed,
            packed,
            packed2,
            edge2,
            edge2,
            edge,
            edge,
            edge,
            edge,
            packed2,
            packed2,
            edge2,
            edge2,
            packed,
            edge,
            edge,
            packed,
            pltpu.VMEM((fields.shape[1], nz, 1, nc), f32),
            pltpu.VMEM((fields.shape[1], nz, 1, nc), f32),
            pltpu.VMEM((nr, vents), f32),
            pltpu.VMEM((nc, vents), f32),
            pltpu.VMEM((nz, vents), f32),
            pltpu.VMEM((nz, vents), f32),
            pltpu.VMEM((1, vents), f32),
            pltpu.VMEM((1, vents), f32),
            pltpu.VMEM((ngy, 1, vents), f32),
            pltpu.VMEM((ngx, 1, vents), f32),
            dma((3, nz // CHUNK)),
            dma((3,)),
            dma((nz,)),
            dma((nz,)),
            dma((N_LONG,)),
            dma((N_LONG,)),
            dma((2, 4)),
            dma((2, 4)),
            dma((3,)),
            dma((3,)),
            dma((ngy + ngx + 1,)),
            dma((ngy + ngx + 1,)),
        ],
        compiler_params=pltpu.CompilerParams(
            collective_id=0, has_side_effects=True, vmem_limit_bytes=58 << 20
        ),
    )(
        fields,
        courant_x,
        courant_y,
        slot_pick,
        horiz_diff,
        vert_diff,
        class_rates,
        vent_cells,
        vent_rate,
        profile,
        precip_class,
        vent_cells.reshape(1, vents),
    )
    return window[None], sums.reshape(vents)


def solution(mesh):
    placed = (
        P("section", None, None, "gx", "gy"),
        P(),
        P(None, "gx", "gy"),
        P(None, "gx", "gy"),
        P(),
        P(),
        P("gx", "gy"),
        P(),
        P(),
        P(),
        P(),
    )
    return jax.shard_map(
        shards,
        mesh=mesh,
        in_specs=placed,
        out_specs=(P("section", None, "gx", "gy"), P()),
        check_vma=False,
    )
```

```python
import jax
import jax.numpy as jnp
from jax import lax
from jax.experimental import pallas as pl
from jax.experimental.pallas import tpu as pltpu
from jax.sharding import PartitionSpec as P

MESH = pl.DeviceIdType.MESH
LANES = 128
CHUNK = 4
GROUPS = 8
SKIP = 2
N_LONG = 3 * GROUPS - SKIP
EARLY = 16
EARLY_ROUNDS = 10
EVERY = 8


def wash_and_slope(conc):
    square = conc * conc
    inverse = 1.0 / (1.0 + square)
    return square * inverse, 2.0 * conc * inverse * inverse


def kernel(
    fields_ref,
    cx_ref,
    cy_ref,
    pick_ref,
    h_ref,
    k_ref,
    rates_ref,
    cells_ref,
    vent_ref,
    prof_ref,
    class_ref,
    where_ref,
    out_ref,
    sums_ref,
    slots,
    c0,
    lam2,
    cx,
    cy,
    state,
    long_buf,
    rate,
    column,
    colsum,
    pack_f,
    pack_c,
    pack_m,
    pack_out,
    edge_hi,
    edge_lo,
    edge_f0,
    edge_c0,
    edge_mhi,
    edge_mlo,
    got_w,
    got_e,
    got_xw,
    got_xe,
    part_p,
    part_hi,
    part_lo,
    halo,
    rows_hi,
    rows_lo,
    hot_x,
    hot_y,
    at_vents,
    from_adjoint,
    term,
    term_in,
    by_gy,
    by_gx,
    ld_sem,
    rw_sem,
    c0_send,
    c0_recv,
    lg_send,
    lg_recv,
    hx_send,
    hx_recv,
    pt_send,
    pt_recv,
    sn_send,
    sn_recv,
):
    nz, nr, nc = c0.shape
    n_chunks = nz // CHUNK
    n_direct = nz - N_LONG
    first_long = 8 * (SKIP // 3) + (1, 4, 6)[SKIP % 3]
    early_direct = EARLY - max(3 * (EARLY // 8) - SKIP, 0)
    s = lax.axis_index("section")
    gx = lax.axis_index("gx")
    gy = lax.axis_index("gy")
    ngx, ngy = lax.axis_size("gx"), lax.axis_size("gy")
    half = (nr, LANES)
    lane = lax.broadcasted_iota(jnp.int32, half, 1)
    row = lax.broadcasted_iota(jnp.int32, half, 0)
    halves = (slice(0, LANES), slice(LANES, 2 * LANES))

    partner = {"section": 1 - s}
    cross = {"section": 1 - s, "gx": gx + 1 - 2 * lax.rem(gx, 2)}
    aside = (
        {"section": 1 - s, "gx": lax.rem(gx + 1, ngx)},
        {"section": 1 - s, "gx": lax.rem(gx + ngx - 1, ngx)},
    )
    beside = (
        {"gy": lax.rem(gy + 1, ngy)},
        {"gy": lax.rem(gy + ngy - 1, ngy)},
        {"gx": lax.rem(gx + 1, ngx)},
        {"gx": lax.rem(gx + ngx - 1, ngx)},
    )

    def remote(src, dst, send, recv, to):
        return pltpu.make_async_remote_copy(
            src, dst, send, recv, device_id=to, device_id_type=MESH
        )

    def chunk(i):
        lead = first_long // CHUNK
        return jnp.where(i == 0, lead, jnp.where(i <= lead, i - 1, i))

    def loads(i):
        at = pl.ds(chunk(i) * CHUNK, CHUNK)
        return (
            pltpu.make_async_copy(fields_ref.at[0, :, at], slots.at[:, at], ld_sem.at[0, i]),
            pltpu.make_async_copy(cx_ref.at[at], cx.at[at], ld_sem.at[1, i]),
            pltpu.make_async_copy(cy_ref.at[at], cy.at[at], ld_sem.at[2, i]),
        )

    def row_loads():
        high, low = pl.ds(nr - 1, 1), pl.ds(0, 1)
        return (
            pltpu.make_async_copy(fields_ref.at[0, :, :, high], rows_hi, rw_sem.at[0]),
            pltpu.make_async_copy(fields_ref.at[0, :, :, low], rows_lo, rw_sem.at[1]),
            pltpu.make_async_copy(cx_ref.at[:, low], edge_c0, rw_sem.at[2]),
        )

    def selected_rows(ref):
        pick = jnp.full(ref.shape[1:], pick_ref[s], jnp.int32)
        a = jnp.where(pick == 0, ref[0], ref[1])
        b = jnp.where(pick == 2, ref[2], ref[3])
        return jnp.where(pick < 2, a, b)

    def direct(z):
        return remote(c0.at[z], c0.at[z], c0_send.at[z], c0_recv.at[z], partner)

    def start_direct(i):
        late = jnp.maximum(i - SKIP, 0)
        r = lax.rem(late, 5)
        paired = 8 * (late // 5) + r + (r + 3) // 4 + r // 3 + r // 4
        direct(jnp.where(i < first_long, i, paired)).start()

    def long_plane(j):
        r = lax.rem(j + SKIP, 3)
        return 8 * ((j + SKIP) // 3) + 1 + 3 * r - r // 2

    def long_one(j):
        z = long_plane(j)
        return remote(c0.at[z], long_buf.at[j], c0_send.at[z], lg_recv.at[j], cross)

    def long_two(j):
        return remote(long_buf.at[j], long_buf.at[j], lg_send.at[j], lg_recv.at[j], partner)

    def long_three(j):
        z = long_plane(j)
        return remote(long_buf.at[j], c0.at[z], lg_send.at[j], c0_recv.at[z], cross)

    def exchange(e):
        return (
            remote(pack_out.at[e], got_w.at[e], hx_send.at[e, 0], hx_recv.at[e, 0], beside[0]),
            remote(pack_out.at[e], got_e.at[e], hx_send.at[e, 1], hx_recv.at[e, 1], beside[1]),
            remote(edge_hi.at[e], got_xw.at[e], hx_send.at[e, 2], hx_recv.at[e, 2], beside[2]),
            remote(edge_lo.at[e], got_xe.at[e], hx_send.at[e, 3], hx_recv.at[e, 3], beside[3]),
        )

    def onward():
        return (
            remote(part_hi, got_xw.at[1], pt_send.at[1], hx_recv.at[1, 2], aside[0]),
            remote(part_lo, got_xe.at[1], pt_send.at[2], hx_recv.at[1, 3], aside[1]),
        )

    def to_partner():
        return (
            remote(pack_out.at[1], part_p, pt_send.at[0], pt_recv.at[0], partner),
            remote(edge_hi.at[1], part_hi, pt_send.at[1], pt_recv.at[1], partner),
            remote(edge_lo.at[1], part_lo, pt_send.at[2], pt_recv.at[2], partner),
        )

    def spread(d):
        to = {"gy": lax.rem(gy + d, ngy)}
        return remote(term, by_gy.at[d - 1], sn_send.at[d - 1], sn_recv.at[d - 1], to)

    def spread_rows(d):
        to = {"gx": lax.rem(gx + d, ngx)}
        i = ngy - 1 + d - 1
        return remote(by_gy.at[ngy - 1], by_gx.at[d - 1], sn_send.at[i], sn_recv.at[i], to)

    def last_sums():
        i = ngy + ngx - 2
        return remote(by_gx.at[ngx - 1], by_gx.at[ngx - 1], sn_send.at[i], sn_recv.at[i], partner)

    def to_forward():
        i = ngy + ngx - 1
        return (
            remote(at_vents, from_adjoint, sn_send.at[i], sn_recv.at[i], partner),
            remote(term, term_in, sn_send.at[i + 1], sn_recv.at[i + 1], partner),
        )

    def prepare_vents():
        cells = where_ref[...]
        width = nc * ngy
        bits = width.bit_length() - 1
        assert width == 1 << bits
        rows = lax.shift_right_logical(cells, bits) - gx * nr
        cols = (cells & (width - 1)) - gy * nc
        hot_x[...] = (lax.broadcasted_iota(jnp.int32, hot_x.shape, 0) == rows).astype(jnp.float32)
        hot_y[...] = (lax.broadcasted_iota(jnp.int32, hot_y.shape, 0) == cols).astype(jnp.float32)

    def vents_of(values):
        found = jnp.dot(
            values.reshape(-1, nc),
            hot_y[...],
            precision=lax.Precision.HIGHEST,
            preferred_element_type=jnp.float32,
        )
        found = found.reshape(-1, nr, hot_x.shape[1]) * hot_x[...][None]
        return jnp.sum(found, 1)

    def gather_vents(ref, weighted, every_other=None):
        @pl.loop(0, nz // 8)
        def _(b):
            z = pl.multiple_of(b * 8, 8)
            found = vents_of(ref[pl.ds(z, 8)])
            if weighted:
                sub = lax.broadcasted_iota(jnp.int32, found.shape, 0)
                weight = jnp.full(found.shape, prof_ref[z], jnp.float32)
                for i in range(1, 8):
                    weight = jnp.where(sub == i, prof_ref[z + i], weight)
                found = found * weight
            at_vents[pl.ds(z, 8), :] = found
            if every_other:
                pl.when(lax.rem(b, 2) == 1)(lambda: every_other(b))

    def finish_exchange(e):
        for copy in exchange(e):
            copy.wait_recv()
        west = jnp.where(gy > 0, 1.0, 0.0)
        east = jnp.where(gy < ngy - 1, 1.0, 0.0)
        low = jnp.where(gx > 0, 1.0, 0.0)
        high = jnp.where(gx < ngx - 1, 1.0, 0.0)
        moved = pltpu.roll(got_e[e], LANES - 2, 1)
        halo[...] = jnp.where(lax.rem(lane, 2) == 0, got_w[e] * west, moved * east)
        got_xw[e] = got_xw[e] * low
        got_xe[e] = got_xe[e] * high

    def pack(ref, z, left, right, *at):
        both = pltpu.roll(jnp.where(lane == LANES - 1, right, left), 2 * z + 1, 1)
        where = (*at, slice(None), slice(None))
        ref[where] = jnp.where(lane // 2 == z, both, ref[where])

    def neighbours(z, e, f, gxs, gys):
        side = pltpu.roll(halo[...], lax.rem(2 * nz - 2 * z, LANES), 1)
        lo = [pltpu.roll(a, 1, 1) for a in f]
        hi = [pltpu.roll(a, LANES - 1, 1) for a in gys]
        south = (jnp.where(lane == 0, side, lo[0]), jnp.where(lane == 0, lo[0], lo[1]))
        north = (
            jnp.where(lane == LANES - 1, hi[1], hi[0]),
            jnp.where(lane == LANES - 1, side, hi[1]),
        )
        below = [got_xw[e, z, :, at] for at in halves]
        above = [got_xe[e, z, :, at] for at in halves]
        west = [jnp.where(row == 0, b, pltpu.roll(a, 1, 0)) for a, b in zip(f, below)]
        east = [jnp.where(row == nr - 1, b, pltpu.roll(a, nr - 1, 0)) for a, b in zip(gxs, above)]
        return west, east, south, north

    def read(ref, z):
        return [ref[z, :, at] for at in halves]

    def vertical(z):
        up, down = jnp.minimum(z + 1, nz - 1), jnp.maximum(z - 1, 0)
        return up, down, jnp.where(z < nz - 1, 1.0, 0.0), jnp.where(z > 0, 1.0, 0.0)

    def forward(src, z, e):
        f, u, v = read(src, z), read(cx, z), read(cy, z)
        h, k = h_ref[z], k_ref[z]
        if e is None:
            west = [pltpu.roll(a, 1, 0) for a in f]
            east = [pltpu.roll(a, nr - 1, 0) for a in f]
            lo = [pltpu.roll(a, 1, 1) for a in f]
            hi = [pltpu.roll(a, LANES - 1, 1) for a in f]
            south = (lo[0], jnp.where(lane == 0, lo[0], lo[1]))
            north = (jnp.where(lane == LANES - 1, hi[1], hi[0]), hi[1])
        else:
            west, east, south, north = neighbours(z, e, f, f, f)
        up, down, has_up, has_down = vertical(z)
        above, below = read(src, up), read(src, down)
        level = 1.0 - 4.0 * h - 2.0 * k
        out = []
        for i, at in enumerate(halves):
            total = (level - u[i] - v[i]) * f[i] + u[i] * west[i] + v[i] * south[i]
            total = total + h * ((west[i] + east[i]) + (south[i] + north[i]))
            total = total + (k * has_up) * above[i] + (k * has_down) * below[i]
            washed, _ = wash_and_slope(f[i])
            out.append(total - rate[:, at] * washed + prof_ref[z] * column[:, at])
        return out

    def transposed(src, z, e):
        f, u, v = read(src, z), read(cx, z), read(cy, z)
        h, k = h_ref[z], k_ref[z]
        qx = [(b + h) * a for a, b in zip(f, u)]
        qy = [(b + h) * a for a, b in zip(f, v)]
        west, east, south, north = neighbours(z, e, f, qx, qy)
        up, down, has_up, has_down = vertical(z)
        above, below = read(src, up), read(src, down)
        k_up, k_down = k_ref[up] * has_up, k_ref[down] * has_down
        level = 1.0 - 4.0 * h - 2.0 * k
        out = []
        for i in range(2):
            total = (level - u[i] - v[i]) * f[i] + east[i] + north[i] + h * (west[i] + south[i])
            out.append(total + k_up * above[i] + k_down * below[i])
        return out

    def selected(z):
        pick = jnp.full(half, pick_ref[s], jnp.int32)
        out = []
        for at in halves:
            a = jnp.where(pick == 0, slots[0, z, :, at], slots[1, z, :, at])
            b = jnp.where(pick == 2, slots[2, z, :, at], slots[3, z, :, at])
            out.append(jnp.where(pick < 2, a, b))
        return out

    def prepare_columns():
        kind = class_ref[...]
        value = jnp.full(kind.shape, rates_ref[0], jnp.float32)
        for c in range(1, rates_ref.shape[0]):
            value = jnp.where(kind == c, rates_ref[c], value)
        rate[...] = value
        column[...] = jnp.zeros_like(column)

        @pl.loop(0, cells_ref.shape[0])
        def _(v):
            column[...] += jnp.where(cell_ids() == cells_ref[v], vent_ref[v], 0.0)

    def cell_ids():
        rows = lax.broadcasted_iota(jnp.int32, (nr, nc), 0) + gx * nr
        return rows * (nc * ngy) + lax.broadcasted_iota(jnp.int32, (nr, nc), 1) + gy * nc

    for copy in (loads(0)[0], *row_loads()):
        copy.start()
    for copy in loads(0)[1:]:
        copy.start()

    @pl.loop(1, n_chunks)
    def _(i):
        for copy in loads(i):
            copy.start()

    barrier = pltpu.get_barrier_semaphore()
    along_gy = [{"gy": lax.rem(gy + d, ngy)} for d in range(1, ngy)]
    along_gx = [{"gx": lax.rem(gx + d, ngx)} for d in range(1, ngx)]
    peers = (partner, *aside, *along_gy, *along_gx)
    for peer in peers:
        pl.semaphore_signal(barrier, 1, device_id=peer, device_id_type=MESH)
    pl.semaphore_wait(barrier, len(peers))

    def send_chunk(i):
        @pl.loop(0, CHUNK)
        def _(t):
            z = chunk(i) * CHUNK + t
            f = selected(z)
            for at, value in zip(halves, f):
                c0[z, :, at] = value
            pack(pack_out, z, f[0], f[1], 0)
            m = lax.rem(z, 8)
            is_long = (z >= first_long) & ((m == 1) | (m == 4) | (m == 6))

            @pl.when(is_long)
            def _():
                long_one(3 * (z // 8) + m // 4 + m // 6 - SKIP).start()

            @pl.when((z < EARLY) & jnp.logical_not(is_long))
            def _():
                direct(z).start()

    @pl.when(s == 0)
    def _():
        loads(0)[0].wait()
        send_chunk(0)

    for copy in row_loads():
        copy.wait()
    edge_hi[0] = selected_rows(rows_hi)
    edge_f0[...] = selected_rows(rows_lo)

    @pl.when(s == 0)
    def _():
        edge_lo[0] = edge_f0[...]

    @pl.when(s == 1)
    def _():
        @pl.loop(0, nz)
        def _(z):
            edge_c0[z] = edge_c0[z] + h_ref[z]

        edge_lo[0] = edge_c0[...] * edge_f0[...]

    for copy in exchange(0)[2:]:
        copy.start()

    @pl.when(s == 0)
    def _():
        def relay(j):
            long_two(j).wait_recv()
            long_three(j).start()

        def round_of(k):
            @pl.when(nz // 16 + k < N_LONG)
            def _():
                relay(nz // 16 + k)

        def pump_from(first, last):
            @pl.loop(first, last)
            def _(k):
                round_of(k)

        @pl.loop(1, n_chunks)
        def _(i):
            for copy in loads(i):
                copy.wait()
            send_chunk(i)

        for copy in exchange(0)[:2]:
            copy.start()
        for copy in loads(0)[1:]:
            copy.wait()
        prepare_columns()
        finish_exchange(0)

        @pl.loop(0, nz)
        def _(z):
            new = forward(c0, z, 0)
            for at, value in zip(halves, new):
                state[z, :, at] = value
                edge_hi[1, z, :, at] = value[nr - 1 : nr]
                edge_lo[1, z, :, at] = value[0:1]
            pack(pack_out, z, new[0], new[1], 1)

            @pl.when(lax.rem(z, 16) == 7)
            def _():
                start_direct(early_direct + z // 16)

            @pl.when(lax.rem(z, 16) == 15)
            def _():
                relay(z // 16)

        for copy in (*to_partner(), *exchange(1)[:2]):
            copy.start()

        @pl.loop(early_direct + nz // 16, n_direct)
        def _(i):
            start_direct(i)

        pump_from(0, EARLY_ROUNDS - 4)
        prepare_vents()
        gather_vents(state, False)
        pump_from(EARLY_ROUNDS - 4, EARLY_ROUNDS)
        finish_exchange(1)

        @pl.loop(0, nz)
        def _(z):
            new = forward(state, z, 1)
            for at, value in zip(halves, new):
                out_ref[z, :, at] = value

            @pl.when(lax.rem(z, EVERY) == EVERY - 1)
            def _():
                round_of(EARLY_ROUNDS + z // EVERY)

        pump_from(EARLY_ROUNDS + nz // EVERY, N_LONG)
        for copy in to_forward():
            copy.wait_recv()
        _, slope = wash_and_slope(at_vents[...])
        lost = jnp.sum(slope * from_adjoint[...], 0, keepdims=True) * vents_of(rate[...])
        term[...] = term_in[...] - lost
        for d in range(1, ngy):
            spread(d).start()
        total = term[...]
        for d in range(1, ngy):
            spread(d).wait_recv()
            total = total + by_gy[d - 1]
        by_gy[ngy - 1] = total
        for d in range(1, ngx):
            spread_rows(d).start()
        for d in range(1, ngx):
            spread_rows(d).wait_recv()
            total = total + by_gx[d - 1]
        by_gx[ngx - 1] = total
        last_sums().start()
        sums_ref[...] = total

        for copy in (*to_partner(), *exchange(0), *exchange(1)[:2], last_sums()):
            copy.wait_send()
        for d in range(1, ngy):
            spread(d).wait_send()
        for d in range(1, ngx):
            spread_rows(d).wait_send()

        @pl.loop(0, nz - 8)
        def _(z):
            direct(z).wait_send()

        @pl.loop(0, N_LONG)
        def _(j):
            long_three(j).wait_send()

        @pl.loop(nz - 8, nz)
        def _(z):
            direct(z).wait_send()

    @pl.when(s == 1)
    def _():
        def relay(j):
            long_one(j).wait_recv()
            long_two(j).start()

        @pl.loop(0, n_chunks)
        def _(i):
            for copy in loads(i):
                copy.wait()

            @pl.loop(0, CHUNK)
            def _(t):
                z = chunk(i) * CHUNK + t
                f = selected(z)
                h = h_ref[z]
                for at, value in zip(halves, f):
                    lam2[z, :, at] = value
                pack(pack_f, z, f[0], f[1])
                pack(pack_c, z, cy[z, :, 0:LANES] + h, jnp.ones(half, jnp.float32))

        pack_out[0] = pack_f[...] * pack_c[...]
        for copy in exchange(0)[:2]:
            copy.start()
        prepare_columns()
        prepare_vents()
        colsum[...] = jnp.zeros_like(colsum)
        finish_exchange(0)

        @pl.loop(0, nz)
        def _(z):
            new = transposed(lam2, z, 0)
            for at, value in zip(halves, new):
                state[z, :, at] = value
                colsum[:, at] += prof_ref[z] * (value + lam2[z, :, at])
                edge_mhi[z, :, at] = value[nr - 1 : nr]
                edge_mlo[z, :, at] = value[0:1]
            pack(pack_m, z, new[0], new[1])

            @pl.when(lax.rem(z, 5) == 4)
            def _():
                relay(z // 5)

        gather_vents(lam2, True, lambda b: relay(12 + b // 2))
        term[...] = vents_of(colsum[...])
        for copy in to_forward():
            copy.start()
        for copy in to_partner():
            copy.wait_recv()
        for copy in onward():
            copy.start()
        _, slope = wash_and_slope(part_hi[...])
        edge_hi[1] = edge_mhi[...] - rate[nr - 1 : nr, :] * slope * edge_hi[0]
        _, slope = wash_and_slope(part_lo[...])
        edge_mlo[...] = edge_mlo[...] - rate[0:1, :] * slope * edge_f0[...]
        edge_lo[1] = edge_mlo[...] * edge_c0[...]
        side_rate = jnp.where(
            lax.rem(lane, 2) == 0,
            jnp.broadcast_to(rate[:, nc - 1 : nc], half),
            jnp.broadcast_to(rate[:, 0:1], half),
        )
        _, slope = wash_and_slope(part_p[...])
        pack_m[...] = pack_m[...] - side_rate * slope * pack_f[...]
        pack_out[1] = pack_m[...] * pack_c[...]
        for copy in exchange(1):
            copy.start()
        for j in range(16, 20):
            relay(j)
        finish_exchange(1)

        def last(z):
            lam = read(state, z)
            new = transposed(state, z, 1)
            conc = read(c0, z)
            for i, at in enumerate(halves):
                _, bend = wash_and_slope(conc[i])
                out_ref[z, :, at] = new[i] - rate[:, at] * bend * lam[i]

        direct(0).wait_recv()

        @pl.loop(0, nz)
        def _(z):
            @pl.when((lax.rem(z, 2) == 0) & (z // 2 < N_LONG - 20))
            def _():
                relay(20 + z // 2)

            @pl.when(z < nz - 1)
            def _():
                direct(z + 1).wait_recv()

            conc = forward(c0, z, None)
            old, field = read(state, z), read(lam2, z)
            sides = pltpu.roll(pack_m[...], lax.rem(2 * nz - 2 * z + LANES - 1, LANES), 1)
            keep = (lane == 0, lane == LANES - 1)
            for i, at in enumerate(halves):
                _, bend = wash_and_slope(conc[i])
                lam = old[i] - rate[:, at] * bend * field[i]
                lam = jnp.where(keep[i], sides, lam)
                lam = jnp.where(row == 0, edge_mlo[z, :, at], lam)
                lam = jnp.where(row == nr - 1, edge_hi[1, z, :, at], lam)
                state[z, :, at] = lam

            @pl.when(z > 0)
            def _():
                last(z - 1)

            @pl.when(z == nz - 6)
            def _():
                @pl.loop(0, N_LONG)
                def _(j):
                    long_two(j).wait_send()

                for copy in (*exchange(0), *exchange(1), *onward(), *to_forward()):
                    copy.wait_send()

        last(nz - 1)
        last_sums().wait_recv()
        sums_ref[...] = by_gx[ngx - 1]


def shards(
    fields,
    slot_pick,
    courant_x,
    courant_y,
    horiz_diff,
    vert_diff,
    precip_class,
    class_rates,
    vent_cells,
    vent_rate,
    profile,
):
    nz, nr, nc = courant_x.shape
    vents = vent_cells.shape[0]
    ngx, ngy = lax.axis_size("gx"), lax.axis_size("gy")
    anywhere = pl.BlockSpec(memory_space=pl.ANY)
    scalars = pl.BlockSpec(memory_space=pltpu.SMEM)
    vector = pl.BlockSpec(memory_space=pltpu.VMEM)
    f32 = jnp.float32
    plane = pltpu.VMEM((nz, nr, nc), f32)
    tile = pltpu.VMEM((nr, nc), f32)
    packed = pltpu.VMEM((nr, LANES), f32)
    edge = pltpu.VMEM((nz, 1, nc), f32)
    packed2 = pltpu.VMEM((2, nr, LANES), f32)
    edge2 = pltpu.VMEM((2, nz, 1, nc), f32)
    dma = pltpu.SemaphoreType.DMA
    window, sums = pl.pallas_call(
        kernel,
        out_shape=(
            pltpu.VMEM((nz, nr, nc), f32),
            jax.ShapeDtypeStruct((1, vents), f32),
        ),
        in_specs=[anywhere] * 3 + [scalars] * 7 + [vector] * 2,
        out_specs=(vector, vector),
        scratch_shapes=[
            pltpu.VMEM((fields.shape[1], nz, nr, nc), f32),
            plane,
            plane,
            plane,
            plane,
            plane,
            pltpu.VMEM((N_LONG, nr, nc), f32),
            tile,
            tile,
            tile,
            packed,
            packed,
            packed,
            packed2,
            edge2,
            edge2,
            edge,
            edge,
            edge,
            edge,
            packed2,
            packed2,
            edge2,
            edge2,
            packed,
            edge,
            edge,
            packed,
            pltpu.VMEM((fields.shape[1], nz, 1, nc), f32),
            pltpu.VMEM((fields.shape[1], nz, 1, nc), f32),
            pltpu.VMEM((nr, vents), f32),
            pltpu.VMEM((nc, vents), f32),
            pltpu.VMEM((nz, vents), f32),
            pltpu.VMEM((nz, vents), f32),
            pltpu.VMEM((1, vents), f32),
            pltpu.VMEM((1, vents), f32),
            pltpu.VMEM((ngy, 1, vents), f32),
            pltpu.VMEM((ngx, 1, vents), f32),
            dma((3, nz // CHUNK)),
            dma((3,)),
            dma((nz,)),
            dma((nz,)),
            dma((N_LONG,)),
            dma((N_LONG,)),
            dma((2, 4)),
            dma((2, 4)),
            dma((3,)),
            dma((3,)),
            dma((ngy + ngx + 1,)),
            dma((ngy + ngx + 1,)),
        ],
        compiler_params=pltpu.CompilerParams(
            collective_id=0, has_side_effects=True, vmem_limit_bytes=58 << 20
        ),
    )(
        fields,
        courant_x,
        courant_y,
        slot_pick,
        horiz_diff,
        vert_diff,
        class_rates,
        vent_cells,
        vent_rate,
        profile,
        precip_class,
        vent_cells.reshape(1, vents),
    )
    return window[None], sums.reshape(vents)


def solution(mesh):
    placed = (
        P("section", None, None, "gx", "gy"),
        P(),
        P(None, "gx", "gy"),
        P(None, "gx", "gy"),
        P(),
        P(),
        P("gx", "gy"),
        P(),
        P(),
        P(),
        P(),
    )
    return jax.shard_map(
        shards,
        mesh=mesh,
        in_specs=placed,
        out_specs=(P("section", None, "gx", "gy"), P()),
        check_vma=False,
    )
```
